32 devices in a mesh: section: 8 (over z, core), seq: 4 (over y, x).
Axes of the slice: x: 2, y: 2, z: 4, core: 2. Of those that a mesh axis runs over, the one named last changes fastest.
Arguments:
- frames_in: bfloat16 [4, 4, 128, 1152], P(None, 'seq'), may hold values from -6 to 6
- spatial_qkv: bfloat16 [8, 1152, 1728], P('section'), may hold values from -0.1875 to 0.1875
- spatial_out: bfloat16 [8, 576, 1152], P('section'), may hold values from -0.25 to 0.25
- temporal_qkv: bfloat16 [8, 1152, 1728], P('section'), may hold values from -0.1875 to 0.1875
- temporal_out: bfloat16 [8, 576, 1152], P('section'), may hold values from -0.25 to 0.25
- modulation: float32 [8, 4, 6, 1152], P('section'), may hold values from -3 to 3
Outputs:
- hidden: bfloat16 [8, 4, 4, 128, 1152], P('section', None, 'seq')
The draws below stay inside these ranges and needn't reach their ends.
All inputs are finite; a program needn't handle non-finite values.
Results may differ from the reference program's by a relative error of at most 0.015.
Values may be sent and summed in bfloat16 or wider, within the bound.
A program may use at most 64 MiB of HBM per device.

```python
import math
import jax
import jax.numpy as jnp
from jax import lax

D = 1152
HEADS = 8
PATCHES = 128
SAMPLES = 4
HW = 576
FRAMES = 4
SECTIONS = 8


def level_of(stream_key, dims, cuts, low, top_value):
    gain = 1.0
    for axis_at, parts in cuts:
        steps = jax.random.uniform(jax.random.fold_in(jax.random.fold_in(stream_key, 6), axis_at), (parts,), jnp.float32, low / len(cuts), top_value / len(cuts))
        gain = gain * jnp.repeat(jnp.exp(steps), dims[axis_at] // parts).reshape((-1,) + (1,) * (len(dims) - 1 - axis_at))
    return gain


def gaussian(own_key, dims, deviation, most, shards=(), kind=jnp.bfloat16):
    level = level_of(own_key, dims, shards, -0.22, 0.18) if shards else 1.0
    array = jax.random.normal(own_key, dims, jnp.float32) * deviation * level
    return jnp.minimum(jnp.maximum(array, -most), most).astype(kind)


def setup_inputs(seed: int = 0) -> dict:
    keys = jax.random.split(jax.random.key(seed), 7)
    frames_in = gaussian(keys[0], (SAMPLES, FRAMES, PATCHES, D), 1.0, 6.0, ((1, 4),))
    spatial_qkv = gaussian(keys[1], (SECTIONS, D, 3 * HW), D ** -0.5, 0.1875, ((0, 8),))
    spatial_out = gaussian(keys[2], (SECTIONS, HW, D), HW ** -0.5, 0.25, ((0, 8),))
    temporal_qkv = gaussian(keys[3], (SECTIONS, D, 3 * HW), D ** -0.5, 0.1875, ((0, 8),))
    temporal_out = gaussian(keys[4], (SECTIONS, HW, D), HW ** -0.5, 0.25, ((0, 8),))
    modulation = gaussian(keys[5], (SECTIONS, SAMPLES, 6, D), 0.5, 3.0, ((0, 8),), jnp.float32)
    return {"frames_in": frames_in, "spatial_qkv": spatial_qkv, "spatial_out": spatial_out, "temporal_qkv": temporal_qkv, "temporal_out": temporal_out, "modulation": modulation}


def norm_modulate(residual, offset, scaling):
    average = lax.optimization_barrier(jnp.mean(residual, axis=-1, keepdims=True))
    centered = residual - average
    variance = lax.optimization_barrier(jnp.mean(centered * centered, axis=-1, keepdims=True))
    return (centered / jnp.sqrt(variance + 1e-06) * (1.0 + scaling) + offset).astype(jnp.bfloat16)

def head_rms(tensor):
    return (tensor / jnp.sqrt(lax.optimization_barrier(jnp.mean(tensor * tensor, axis=-1, keepdims=True)) + 1e-06)).astype(jnp.bfloat16)

def split_heads(projected, head_count):
    head_width = projected.shape[-1] // 3
    heads_shape = projected.shape[:-1] + (head_count, head_width // head_count)
    queries = head_rms(projected[..., :head_width].reshape(heads_shape))
    lookups = head_rms(projected[..., head_width:2 * head_width].reshape(heads_shape))
    values = projected[..., 2 * head_width:].reshape(heads_shape).astype(jnp.bfloat16)
    return (queries, lookups, values)

def merge_heads(tensor):
    return tensor.reshape(tensor.shape[:-2] + (tensor.shape[-2] * tensor.shape[-1],))

def attend(queries, lookups, values):
    queries, lookups, values = lax.optimization_barrier((queries, lookups, values))
    scores = jnp.einsum('...qhd,...khd->...hqk', queries.astype(jnp.float32), lookups.astype(jnp.float32))
    scores = scores / math.sqrt(queries.shape[-1])
    exponent = jnp.exp(scores)
    totals = lax.optimization_barrier(jnp.sum(exponent, axis=-1))
    rounded = lax.optimization_barrier(exponent.astype(jnp.bfloat16))
    mixed = jnp.einsum('...hqk,...khd->...qhd', rounded.astype(jnp.float32), values.astype(jnp.float32))
    return (mixed / jnp.swapaxes(totals, -1, -2)[..., None]).astype(jnp.bfloat16)

def reference(frames_in, spatial_qkv, spatial_out, temporal_qkv, temporal_out, modulation):
    residual = frames_in.astype(jnp.float32)
    outputs = []
    for section_index in range(SECTIONS):
        factors = modulation[section_index][:, :, None, None, :]
        normed = norm_modulate(residual, factors[:, 0], factors[:, 1])
        projected = jnp.dot(normed, spatial_qkv[section_index], preferred_element_type=jnp.float32)
        queries, lookups, values = split_heads(projected, HEADS)
        mixed = merge_heads(attend(queries, lookups, values))
        middle = residual + factors[:, 2] * jnp.dot(mixed, spatial_out[section_index], preferred_element_type=jnp.float32)
        normed = norm_modulate(middle, factors[:, 3], factors[:, 4])
        projected = jnp.dot(normed, temporal_qkv[section_index], preferred_element_type=jnp.float32)
        queries, lookups, values = split_heads(projected, HEADS)
        mixed = attend(jnp.swapaxes(queries, 1, 2), jnp.swapaxes(lookups, 1, 2), jnp.swapaxes(values, 1, 2))
        mixed = merge_heads(jnp.swapaxes(mixed, 1, 2))
        updated = middle + factors[:, 5] * jnp.dot(mixed, temporal_out[section_index], preferred_element_type=jnp.float32)
        updated = lax.optimization_barrier(updated.astype(jnp.bfloat16))
        outputs.append(updated)
        residual = updated.astype(jnp.float32)
    return jnp.stack(outputs)
```

```python
import functools
import math

import jax
import jax.numpy as jnp
from jax import lax
from jax.experimental import pallas as pl
from jax.experimental.pallas import tpu as pltpu
from jax.sharding import PartitionSpec as P

HEADS = 8
LANES = 128
CHUNK = 256
MESH = pl.DeviceIdType.MESH


def chunks(width, size=CHUNK):
    return [(at, min(at + size, width)) for at in range(0, width, size)]


def head_windows(head_width):
    size = head_width // HEADS
    found = []
    for pair in range(HEADS // 2):
        low, high = 2 * pair * size, 2 * (pair + 1) * size
        start = low // LANES * LANES
        stop = min(head_width, -(-high // LANES) * LANES)
        found.append((start, stop, low, low + size, high))
    return found


def gather_windows(head_width, parts):
    columns = []
    for low, high in chunks(head_width, LANES):
        total = None
        for (start, stop), part in parts:
            if start <= low and high <= stop:
                piece = part[:, low - start : high - start]
                total = piece if total is None else total + piece
        columns.append(total)
    return jnp.concatenate(columns, axis=1)


def flipped(index, step, count):
    total, bit = 0, 1
    while bit < count:
        total = total + lax.rem(index // bit + step // bit, 2) * bit
        bit *= 2
    return total


def norm_modulate(residual, offset, scaling):
    centered = residual - jnp.mean(residual, axis=-1, keepdims=True)
    variance = jnp.mean(centered * centered, axis=-1, keepdims=True)
    return centered * lax.rsqrt(variance + 1e-06) * (1.0 + scaling) + offset


def split_rows(tensor, count):
    rows = tensor.shape[0] // count
    return [tensor[r * rows : (r + 1) * rows].astype(jnp.bfloat16) for r in range(count)]


def join_rows(ref, sample):
    _, count, rows, width = ref.shape
    if rows % 16 == 0:
        return ref[sample].reshape(count * rows, width)
    parts = [ref[sample, r].astype(jnp.float32) for r in range(count)]
    return jnp.concatenate(parts, axis=0).astype(jnp.bfloat16)


def kernel(
    seq_count, sections,
    frames_hbm, sqkv_hbm, sout_hbm, tqkv_hbm, tout_hbm, mod_hbm,
    hidden_hbm,
    sqkv, sout, tqkv, tout, mod, factors, sqkv_across, tqkv_across, tout_before, gate_before, gates,
    x_in, x_out, y_out, residual, middle, qkv, sent, arrived, mixed_sent, returned, handed,
    pair_mask, square_mask, patch_mask,
    load_sem, frame_sem, store_sem, lend_send, lend_recv,
    hop_send, hop_recv, go_send, go_recv, back_send, back_recv, ahead_send, ahead_recv,
    home_send, home_recv,
):
    samples, patches, width = x_in.shape
    head_width = sout.shape[0]
    head_size = head_width // HEADS
    windows = head_windows(head_width)
    section = lax.axis_index("section")
    me = lax.axis_index("seq")

    loads = [
        pltpu.make_async_copy(src.at[0], dst, load_sem.at[at])
        for at, (src, dst) in enumerate(
            ((mod_hbm, mod), (sqkv_hbm, sqkv), (sout_hbm, sout), (tqkv_hbm, tqkv), (tout_hbm, tout))
        )
    ]

    def frame_load(sample):
        return pltpu.make_async_copy(
            frames_hbm.at[sample], x_in.at[sample], frame_sem.at[sample]
        )

    @pl.when(section == 0)
    def _():
        frame_load(0).start()

    loads[0].start()
    loads[1].start()

    @pl.when(section == 0)
    def _():
        for sample in range(1, samples):
            frame_load(sample).start()

    for load in loads[2:]:
        load.start()

    barrier = pltpu.get_barrier_semaphore()
    for step in range(1, seq_count):
        pl.semaphore_signal(
            barrier, inc=1, device_id={"seq": flipped(me, step, seq_count)}, device_id_type=MESH
        )
    for step in (1, sections - 1):
        for other in range(seq_count):
            pl.semaphore_signal(
                barrier, inc=1,
                device_id={"section": lax.rem(section + step, sections), "seq": other},
                device_id_type=MESH,
            )

    for at, (start, stop, low, center, high) in enumerate(windows):
        span = stop - start
        lane = lax.broadcasted_iota(jnp.int32, (2 * patches, span), 1) + start
        row = lax.broadcasted_iota(jnp.int32, (2 * patches, span), 0)
        first = jnp.where((lane >= low) & (lane < center), 1.0, 0.0)
        second = jnp.where((lane >= center) & (lane < high), 1.0, 0.0)
        pair_mask[at, :, :span] = jnp.where(row < patches, first, second).astype(jnp.bfloat16)
        lane = lax.broadcasted_iota(jnp.int32, (span, span), 1) + start
        row = lax.broadcasted_iota(jnp.int32, (span, span), 0) + start
        first = (lane >= low) & (lane < center) & (row >= low) & (row < center)
        second = (lane >= center) & (lane < high) & (row >= center) & (row < high)
        square_mask[at, :span, :span] = jnp.where(
            first, 1.0, jnp.where(second, 1.0, 0.0)
        ).astype(jnp.bfloat16)
    group = patches // seq_count
    row = lax.broadcasted_iota(jnp.int32, (patches, 2 * patches), 0)
    lane = lax.broadcasted_iota(jnp.int32, (patches, 2 * patches), 1)
    patch_mask[...] = jnp.where(
        lax.rem(row, group) == lax.rem(lane, group), 1.0, 0.0
    ).astype(jnp.bfloat16)

    pl.semaphore_wait(barrier, seq_count - 1 + 2 * seq_count)

    def following(seq=None):
        place = {"section": lax.rem(section + 1, sections)}
        if seq is not None:
            place["seq"] = seq
        return place

    lends = [
        pltpu.make_async_remote_copy(
            src_ref=src, dst_ref=dst, send_sem=lend_send.at[at], recv_sem=lend_recv.at[at],
            device_id=following(), device_id_type=MESH,
        )
        for at, (src, dst) in enumerate(
            ((tout_hbm.at[0], tout_before), (mod_hbm.at[0, mod.shape[0] - 1], gate_before))
        )
    ]

    @pl.when(section < sections - 1)
    def _():
        for lend in lends:
            lend.start()

    def turn(load, stored, across):
        load.wait()
        for low, high in chunks(3 * head_width):
            across[:, low:high] = stored[low:high, :].T

    turn(loads[1], sqkv, sqkv_across)

    @pl.when(section > 0)
    def _():
        turn(loads[3], tqkv, tqkv_across)

    def factor(sample, row, low=0, high=width):
        return factors[sample, row : row + 1, low:high]

    def project(rows, across):
        for low, high in chunks(3 * head_width):
            qkv[:, low:high] = jnp.dot(
                rows, across[:, low:high], preferred_element_type=jnp.float32
            )

    def attend(same_patch):
        queries = qkv[:, :head_width]
        aligned = head_width // LANES * LANES
        lookups = qkv[:, aligned : 2 * head_width]
        if aligned != head_width:
            reach = 2 * head_width - aligned
            lookups = pltpu.roll(lookups, reach - (head_width - aligned), 1)[:, :head_width]
        values = qkv[:, 2 * head_width :].astype(jnp.bfloat16)
        squares = jnp.concatenate([queries * queries, lookups * lookups], axis=0)
        squares = squares.astype(jnp.bfloat16)
        parts = []
        for at, (start, stop, *_) in enumerate(windows):
            span = stop - start
            parts.append(((start, stop), jnp.dot(
                squares[:, start:stop], square_mask[at, :span, :span],
                preferred_element_type=jnp.float32,
            )))
        norms = lax.rsqrt(gather_windows(head_width, parts) * (1.0 / head_size) + 1e-06)
        scale = math.log2(math.e) / math.sqrt(head_size)
        queries = (queries * (norms[:patches] * scale)).astype(jnp.bfloat16)
        lookups = (lookups * norms[patches:]).astype(jnp.bfloat16)
        tops, bottoms = [], []
        for at, (start, stop, *_) in enumerate(windows):
            mask = pair_mask[at, :, : stop - start]
            part = lookups[:, start:stop]
            both = jnp.concatenate([part, part], axis=0) * mask
            scores = lax.dot_general(
                queries[:, start:stop], both, (((1,), (1,)), ((), ())),
                preferred_element_type=jnp.float32,
            )
            exponent = jnp.exp2(scores).astype(jnp.bfloat16)
            if same_patch:
                exponent = exponent * patch_mask[...]
            part = values[:, start:stop]
            both = jnp.concatenate([part, part], axis=0) * mask
            tops.append(((start, stop), jnp.dot(
                exponent, both, preferred_element_type=jnp.float32
            )))
            bottoms.append(((start, stop), jnp.dot(
                exponent, mask, preferred_element_type=jnp.float32
            )))
        return gather_windows(head_width, tops) / gather_windows(head_width, bottoms)

    def exchange(source, target, send_sem, recv_sem, sample, step):
        peer = flipped(me, step, seq_count)
        return pltpu.make_async_remote_copy(
            src_ref=source.at[sample, peer],
            dst_ref=target.at[sample, me],
            send_sem=send_sem.at[sample, step],
            recv_sem=recv_sem.at[sample, step],
            device_id={"seq": peer},
            device_id_type=MESH,
        )

    def go(sample, step):
        return exchange(sent, arrived, go_send, go_recv, sample, step)

    def back(sample, step):
        return exchange(mixed_sent, returned, back_send, back_recv, sample, step)

    def hop(sample):
        return pltpu.make_async_remote_copy(
            src_ref=y_out.at[sample],
            dst_ref=x_in.at[sample],
            send_sem=hop_send.at[sample],
            recv_sem=hop_recv.at[sample],
            device_id=following(),
            device_id_type=MESH,
        )

    def ahead(sample, step):
        peer = flipped(me, step, seq_count)
        return pltpu.make_async_remote_copy(
            src_ref=mixed_sent.at[sample, peer],
            dst_ref=handed.at[sample, me],
            send_sem=ahead_send.at[sample, step],
            recv_sem=ahead_recv.at[sample, step],
            device_id=following(peer),
            device_id_type=MESH,
        )

    def home(sample):
        return pltpu.make_async_remote_copy(
            src_ref=x_out.at[sample],
            dst_ref=hidden_hbm.at[sample],
            send_sem=home_send.at[sample],
            recv_sem=home_recv.at[sample],
            device_id={"section": lax.rem(section + sections - 1, sections)},
            device_id_type=MESH,
        )

    def store(sample):
        return pltpu.make_async_copy(
            y_out.at[sample], hidden_hbm.at[sample], store_sem.at[sample]
        )

    steps = range(seq_count - 1, 0, -1)
    every = range(seq_count - 1, -1, -1)

    def spatial(sample):
        @pl.when(sample == 0)
        def _():
            loads[0].wait()
            for video in range(samples):
                for row in range(mod.shape[0]):
                    factors[video, row : row + 1, :] = mod[row, video : video + 1, :]

        @pl.when(section == 0)
        def _():
            frame_load(sample).wait()
            residual[...] = x_in[sample].astype(jnp.float32)

        @pl.when(section > 0)
        def _():
            @pl.when(sample == 0)
            def _():
                for lend in lends:
                    lend.wait_recv()
                for video in range(samples):
                    gates[video] = gate_before[video : video + 1, :]

            hop(sample).wait_recv()
            for step in every:
                ahead(sample, step).wait_recv()
            mixed = join_rows(handed, sample)
            for low, high in chunks(width):
                residual[:, low:high] = x_in[sample, :, low:high].astype(jnp.float32) + gates[
                    sample, :, low:high
                ] * jnp.dot(mixed, tout_before[:, low:high], preferred_element_type=jnp.float32)

        normed = norm_modulate(residual[...], factor(sample, 0), factor(sample, 1))
        project(normed.astype(jnp.bfloat16), sqkv_across)
        mixed = attend(False).astype(jnp.bfloat16)

        @pl.when(sample == 0)
        def _():
            loads[2].wait()

        for low, high in chunks(width):
            middle[sample, :, low:high] = residual[:, low:high] + factor(
                sample, 2, low, high
            ) * jnp.dot(mixed, sout[:, low:high], preferred_element_type=jnp.float32)
        payload = norm_modulate(middle[sample], factor(sample, 3), factor(sample, 4))
        for at, part in enumerate(split_rows(payload, seq_count)):
            sent[sample, at] = part
        for step in steps:
            go(sample, step).start()
        arrived[sample, me] = sent[sample, me]
        y_out[sample] = middle[sample].astype(jnp.bfloat16)

        @pl.when(section < sections - 1)
        def _():
            hop(sample).start()

        @pl.when(section > 0)
        def _():
            x_out[sample] = residual[...].astype(jnp.bfloat16)
            home(sample).start()

    def temporal(sample):
        for step in steps:
            go(sample, step).wait_recv()
        project(join_rows(arrived, sample), tqkv_across)
        for at, part in enumerate(split_rows(attend(True), seq_count)):
            mixed_sent[sample, at] = part

        @pl.when(section < sections - 1)
        def _():
            for step in every:
                ahead(sample, step).start()

        @pl.when(section == sections - 1)
        def _():
            for step in steps:
                back(sample, step).start()
            returned[sample, me] = mixed_sent[sample, me]

    def finish(sample):
        @pl.when(sample == 0)
        def _():
            loads[4].wait()

        for step in steps:
            back(sample, step).wait_recv()
        mixed = join_rows(returned, sample)
        for low, high in chunks(width):
            y_out[sample, :, low:high] = (
                middle[sample, :, low:high]
                + factor(sample, 5, low, high)
                * jnp.dot(mixed, tout[:, low:high], preferred_element_type=jnp.float32)
            ).astype(jnp.bfloat16)

        store(sample).start()

    @pl.loop(0, samples + 2)
    def _(at):
        @pl.when(at < samples)
        def _():
            spatial(at)

        @pl.when((at == 0) & (section == 0))
        def _():
            turn(loads[3], tqkv, tqkv_across)

        @pl.when((at > 0) & (at <= samples))
        def _():
            temporal(at - 1)

        @pl.when((at > 1) & (section == sections - 1))
        def _():
            finish(at - 2)

    for sample in range(samples):
        for step in steps:
            go(sample, step).wait_send()

    @pl.when(section > 0)
    def _():
        for sample in range(samples):
            home(sample).wait_send()

    @pl.when(section < sections - 1)
    def _():
        loads[4].wait()
        for sample in range(samples):
            hop(sample).wait_send()
            for step in every:
                ahead(sample, step).wait_send()
            home(sample).wait_recv()
        for lend in lends:
            lend.wait_send()

    @pl.when(section == sections - 1)
    def _():
        for sample in range(samples):
            for step in steps:
                back(sample, step).wait_send()
            store(sample).wait()


def on_device(frames_in, spatial_qkv, spatial_out, temporal_qkv, temporal_out, modulation):
    samples, local_frames, patches, width = frames_in.shape
    assert local_frames == 1
    seq_count = lax.axis_size("seq")
    sections = lax.axis_size("section")
    head_width = spatial_out.shape[1]
    rows = patches // seq_count
    bf16, f32 = jnp.bfloat16, jnp.float32
    dma = pltpu.SemaphoreType.DMA
    anywhere = pl.BlockSpec(memory_space=pltpu.HBM)
    span = max(stop - start for start, stop, *_ in head_windows(head_width))
    hidden = pl.pallas_call(
        functools.partial(kernel, seq_count, sections),
        out_shape=jax.ShapeDtypeStruct((samples, patches, width), bf16),
        in_specs=[anywhere] * 6,
        out_specs=anywhere,
        scratch_shapes=[
            pltpu.VMEM(spatial_qkv.shape[:0:-1], bf16),
            pltpu.VMEM(spatial_out.shape[1:], bf16),
            pltpu.VMEM(temporal_qkv.shape[:0:-1], bf16),
            pltpu.VMEM(temporal_out.shape[1:], bf16),
            pltpu.VMEM((modulation.shape[2], samples, width), f32),
            pltpu.VMEM((samples, modulation.shape[2], width), f32),
            pltpu.VMEM(spatial_qkv.shape[1:], bf16),
            pltpu.VMEM(temporal_qkv.shape[1:], bf16),
            pltpu.VMEM(temporal_out.shape[1:], bf16),
            pltpu.VMEM((samples, width), f32),
            pltpu.VMEM((samples, 1, width), f32),
            pltpu.VMEM((samples, patches, width), bf16),
            pltpu.VMEM((samples, patches, width), bf16),
            pltpu.VMEM((samples, patches, width), bf16),
            pltpu.VMEM((patches, width), f32),
            pltpu.VMEM((samples, patches, width), f32),
            pltpu.VMEM((patches, 3 * head_width), f32),
            pltpu.VMEM((samples, seq_count, rows, width), bf16),
            pltpu.VMEM((samples, seq_count, rows, width), bf16),
            pltpu.VMEM((samples, seq_count, rows, head_width), bf16),
            pltpu.VMEM((samples, seq_count, rows, head_width), bf16),
            pltpu.VMEM((samples, seq_count, rows, head_width), bf16),
            pltpu.VMEM((HEADS // 2, 2 * patches, span), bf16),
            pltpu.VMEM((HEADS // 2, span, span), bf16),
            pltpu.VMEM((patches, 2 * patches), bf16),
            dma((5,)),
            dma((samples,)),
            dma((samples,)),
            dma((2,)),
            dma((2,)),
            dma((samples,)),
            dma((samples,)),
            dma((samples, seq_count)),
            dma((samples, seq_count)),
            dma((samples, seq_count)),
            dma((samples, seq_count)),
            dma((samples, seq_count)),
            dma((samples, seq_count)),
            dma((samples,)),
            dma((samples,)),
        ],
        compiler_params=pltpu.CompilerParams(
            collective_id=0, has_side_effects=True, vmem_limit_bytes=60 * 1024 * 1024
        ),
    )(
        frames_in.reshape(samples, patches, width),
        jnp.swapaxes(spatial_qkv, 1, 2), spatial_out,
        jnp.swapaxes(temporal_qkv, 1, 2), temporal_out,
        jnp.swapaxes(modulation, 1, 2),
    )
    return hidden.reshape(1, samples, 1, patches, width)


def solution(mesh):
    placed = (
        P(None, "seq", None, None),
        P("section", None, None),
        P("section", None, None),
        P("section", None, None),
        P("section", None, None),
        P("section", None, None, None),
    )
    return jax.shard_map(
        on_device,
        mesh=mesh,
        in_specs=placed,
        out_specs=P("section", None, "seq", None, None),
        check_vma=False,
    )
```

```python
import functools
import math

import jax
import jax.numpy as jnp
from jax import lax
from jax.experimental import pallas as pl
from jax.experimental.pallas import tpu as pltpu
from jax.sharding import PartitionSpec as P

HEADS = 8
LANES = 128
CHUNK = 256
MESH = pl.DeviceIdType.MESH


def chunks(width, size=CHUNK):
    return [(at, min(at + size, width)) for at in range(0, width, size)]


def head_windows(head_width):
    size = head_width // HEADS
    found = []
    for pair in range(HEADS // 2):
        low, high = 2 * pair * size, 2 * (pair + 1) * size
        start = low // LANES * LANES
        stop = min(head_width, -(-high // LANES) * LANES)
        found.append((start, stop, low, low + size, high))
    return found


def gather_windows(head_width, parts):
    columns = []
    for low, high in chunks(head_width, LANES):
        total = None
        for (start, stop), part in parts:
            if start <= low and high <= stop:
                piece = part[:, low - start : high - start]
                total = piece if total is None else total + piece
        columns.append(total)
    return jnp.concatenate(columns, axis=1)


def flipped(index, step, count):
    total, bit = 0, 1
    while bit < count:
        total = total + lax.rem(index // bit + step // bit, 2) * bit
        bit *= 2
    return total


def norm_modulate(residual, offset, scaling):
    centered = residual - jnp.mean(residual, axis=-1, keepdims=True)
    variance = jnp.mean(centered * centered, axis=-1, keepdims=True)
    return centered * lax.rsqrt(variance + 1e-06) * (1.0 + scaling) + offset


def split_rows(tensor, count):
    rows = tensor.shape[0] // count
    return [tensor[r * rows : (r + 1) * rows].astype(jnp.bfloat16) for r in range(count)]


def join_rows(ref, sample):
    _, count, rows, width = ref.shape
    if rows % 16 == 0:
        return ref[sample].reshape(count * rows, width)
    parts = [ref[sample, r].astype(jnp.float32) for r in range(count)]
    return jnp.concatenate(parts, axis=0).astype(jnp.bfloat16)


def kernel(
    seq_count, sections,
    frames_hbm, sqkv_hbm, sout_hbm, tqkv_hbm, tout_hbm, mod_hbm,
    hidden_hbm,
    sqkv, sout, tqkv, tout, mod, factors, sqkv_across, tqkv_across, tout_before, gate_before, gates,
    x_in, x_out, y_out, residual, middle, qkv, sent, arrived, mixed_sent, returned, handed,
    pair_mask, square_mask, patch_mask,
    load_sem, frame_sem, store_sem, lend_send, lend_recv,
    hop_send, hop_recv, go_send, go_recv, back_send, back_recv, ahead_send, ahead_recv,
    home_send, home_recv,
):
    samples, patches, width = x_in.shape
    head_width = sout.shape[0]
    head_size = head_width // HEADS
    windows = head_windows(head_width)
    section = lax.axis_index("section")
    me = lax.axis_index("seq")

    loads = [
        pltpu.make_async_copy(src.at[0], dst, load_sem.at[at])
        for at, (src, dst) in enumerate(
            ((mod_hbm, mod), (sqkv_hbm, sqkv), (sout_hbm, sout), (tqkv_hbm, tqkv), (tout_hbm, tout))
        )
    ]

    def frame_load(sample):
        return pltpu.make_async_copy(
            frames_hbm.at[sample], x_in.at[sample], frame_sem.at[sample]
        )

    @pl.when(section == 0)
    def _():
        frame_load(0).start()

    loads[0].start()
    loads[1].start()

    barrier = pltpu.get_barrier_semaphore()
    for step in range(1, seq_count):
        pl.semaphore_signal(
            barrier, inc=1, device_id={"seq": flipped(me, step, seq_count)}, device_id_type=MESH
        )
    def greet(step):
        for other in range(seq_count):
            pl.semaphore_signal(
                barrier, inc=1,
                device_id={"section": section + step, "seq": other}, device_id_type=MESH,
            )

    @pl.when(section > 0)
    def _():
        greet(-1)

    @pl.when(section < sections - 1)
    def _():
        greet(1)

    for at, (start, stop, low, center, high) in enumerate(windows):
        span = stop - start
        lane = lax.broadcasted_iota(jnp.int32, (2 * patches, span), 1) + start
        row = lax.broadcasted_iota(jnp.int32, (2 * patches, span), 0)
        first = jnp.where((lane >= low) & (lane < center), 1.0, 0.0)
        second = jnp.where((lane >= center) & (lane < high), 1.0, 0.0)
        pair_mask[at, :, :span] = jnp.where(row < patches, first, second).astype(jnp.bfloat16)
        lane = lax.broadcasted_iota(jnp.int32, (span, span), 1) + start
        row = lax.broadcasted_iota(jnp.int32, (span, span), 0) + start
        first = (lane >= low) & (lane < center) & (row >= low) & (row < center)
        second = (lane >= center) & (lane < high) & (row >= center) & (row < high)
        square_mask[at, :span, :span] = jnp.where(
            first, 1.0, jnp.where(second, 1.0, 0.0)
        ).astype(jnp.bfloat16)
    group = patches // seq_count
    row = lax.broadcasted_iota(jnp.int32, (patches, 2 * patches), 0)
    lane = lax.broadcasted_iota(jnp.int32, (patches, 2 * patches), 1)
    patch_mask[...] = jnp.where(
        lax.rem(row, group) == lax.rem(lane, group), 1.0, 0.0
    ).astype(jnp.bfloat16)

    def turn(load, stored, across):
        load.wait()
        for low, high in chunks(3 * head_width):
            across[:, low:high] = stored[low:high, :].T

    turn(loads[1], sqkv, sqkv_across)
    for load in loads[2:]:
        load.start()

    @pl.when(section == 0)
    def _():
        for sample in range(1, samples):
            frame_load(sample).start()

    beside = jnp.minimum(section, 1) + jnp.minimum(sections - 1 - section, 1)
    pl.semaphore_wait(barrier, seq_count - 1 + seq_count * beside)

    def following(seq=None):
        place = {"section": lax.rem(section + 1, sections)}
        if seq is not None:
            place["seq"] = seq
        return place

    lends = [
        pltpu.make_async_remote_copy(
            src_ref=src, dst_ref=dst, send_sem=lend_send.at[at], recv_sem=lend_recv.at[at],
            device_id=following(), device_id_type=MESH,
        )
        for at, (src, dst) in enumerate(
            ((tout_hbm.at[0], tout_before), (mod_hbm.at[0, mod.shape[0] - 1], gate_before))
        )
    ]

    @pl.when(section < sections - 1)
    def _():
        for lend in lends:
            lend.start()

    @pl.when(section > 0)
    def _():
        turn(loads[3], tqkv, tqkv_across)

    def factor(sample, row, low=0, high=width):
        return factors[sample, row : row + 1, low:high]

    def project(rows, across):
        for low, high in chunks(3 * head_width):
            qkv[:, low:high] = jnp.dot(
                rows, across[:, low:high], preferred_element_type=jnp.float32
            )

    def attend(same_patch):
        queries = qkv[:, :head_width]
        aligned = head_width // LANES * LANES
        lookups = qkv[:, aligned : 2 * head_width]
        if aligned != head_width:
            reach = 2 * head_width - aligned
            lookups = pltpu.roll(lookups, reach - (head_width - aligned), 1)[:, :head_width]
        values = qkv[:, 2 * head_width :].astype(jnp.bfloat16)
        squares = jnp.concatenate([queries * queries, lookups * lookups], axis=0)
        squares = squares.astype(jnp.bfloat16)
        parts = []
        for at, (start, stop, *_) in enumerate(windows):
            span = stop - start
            parts.append(((start, stop), jnp.dot(
                squares[:, start:stop], square_mask[at, :span, :span],
                preferred_element_type=jnp.float32,
            )))
        norms = lax.rsqrt(gather_windows(head_width, parts) * (1.0 / head_size) + 1e-06)
        scale = math.log2(math.e) / math.sqrt(head_size)
        queries = (queries * (norms[:patches] * scale)).astype(jnp.bfloat16)
        lookups = (lookups * norms[patches:]).astype(jnp.bfloat16)
        tops, bottoms = [], []
        for at, (start, stop, *_) in enumerate(windows):
            mask = pair_mask[at, :, : stop - start]
            part = lookups[:, start:stop]
            both = jnp.concatenate([part, part], axis=0) * mask
            scores = lax.dot_general(
                queries[:, start:stop], both, (((1,), (1,)), ((), ())),
                preferred_element_type=jnp.float32,
            )
            exponent = jnp.exp2(scores).astype(jnp.bfloat16)
            if same_patch:
                exponent = exponent * patch_mask[...]
            part = values[:, start:stop]
            both = jnp.concatenate([part, part], axis=0) * mask
            tops.append(((start, stop), jnp.dot(
                exponent, both, preferred_element_type=jnp.float32
            )))
            bottoms.append(((start, stop), jnp.dot(
                exponent, mask, preferred_element_type=jnp.float32
            )))
        return gather_windows(head_width, tops) / gather_windows(head_width, bottoms)

    def exchange(source, target, send_sem, recv_sem, sample, step):
        peer = flipped(me, step, seq_count)
        return pltpu.make_async_remote_copy(
            src_ref=source.at[sample, peer],
            dst_ref=target.at[sample, me],
            send_sem=send_sem.at[sample, step],
            recv_sem=recv_sem.at[sample, step],
            device_id={"seq": peer},
            device_id_type=MESH,
        )

    def go(sample, step):
        return exchange(sent, arrived, go_send, go_recv, sample, step)

    def back(sample, step):
        return exchange(mixed_sent, returned, back_send, back_recv, sample, step)

    def hop(sample):
        return pltpu.make_async_remote_copy(
            src_ref=y_out.at[sample],
            dst_ref=x_in.at[sample],
            send_sem=hop_send.at[sample],
            recv_sem=hop_recv.at[sample],
            device_id=following(),
            device_id_type=MESH,
        )

    def ahead(sample, step):
        peer = flipped(me, step, seq_count)
        return pltpu.make_async_remote_copy(
            src_ref=mixed_sent.at[sample, peer],
            dst_ref=handed.at[sample, me],
            send_sem=ahead_send.at[sample, step],
            recv_sem=ahead_recv.at[sample, step],
            device_id=following(peer),
            device_id_type=MESH,
        )

    def home(sample):
        return pltpu.make_async_remote_copy(
            src_ref=x_out.at[sample],
            dst_ref=hidden_hbm.at[sample],
            send_sem=home_send.at[sample],
            recv_sem=home_recv.at[sample],
            device_id={"section": lax.rem(section + sections - 1, sections)},
            device_id_type=MESH,
        )

    def store(sample):
        return pltpu.make_async_copy(
            y_out.at[sample], hidden_hbm.at[sample], store_sem.at[sample]
        )

    steps = range(seq_count - 1, 0, -1)
    every = range(seq_count - 1, -1, -1)

    def spatial(sample):
        @pl.when(sample == 0)
        def _():
            loads[0].wait()
            for video in range(samples):
                for row in range(mod.shape[0]):
                    factors[video, row : row + 1, :] = mod[row, video : video + 1, :]

        @pl.when(section == 0)
        def _():
            frame_load(sample).wait()
            residual[...] = x_in[sample].astype(jnp.float32)

        @pl.when(section > 0)
        def _():
            @pl.when(sample == 0)
            def _():
                for lend in lends:
                    lend.wait_recv()
                for video in range(samples):
                    gates[video] = gate_before[video : video + 1, :]

            hop(sample).wait_recv()
            for step in every:
                ahead(sample, step).wait_recv()
            mixed = join_rows(handed, sample)
            for low, high in chunks(width):
                residual[:, low:high] = x_in[sample, :, low:high].astype(jnp.float32) + gates[
                    sample, :, low:high
                ] * jnp.dot(mixed, tout_before[:, low:high], preferred_element_type=jnp.float32)

        normed = norm_modulate(residual[...], factor(sample, 0), factor(sample, 1))
        project(normed.astype(jnp.bfloat16), sqkv_across)
        mixed = attend(False).astype(jnp.bfloat16)

        @pl.when(sample == 0)
        def _():
            loads[2].wait()

        for low, high in chunks(width):
            middle[sample, :, low:high] = residual[:, low:high] + factor(
                sample, 2, low, high
            ) * jnp.dot(mixed, sout[:, low:high], preferred_element_type=jnp.float32)
        payload = norm_modulate(middle[sample], factor(sample, 3), factor(sample, 4))
        for at, part in enumerate(split_rows(payload, seq_count)):
            sent[sample, at] = part
        for step in steps:
            go(sample, step).start()
        arrived[sample, me] = sent[sample, me]
        y_out[sample] = middle[sample].astype(jnp.bfloat16)

        @pl.when(section > 0)
        def _():
            x_out[sample] = residual[...].astype(jnp.bfloat16)

    def temporal(sample):
        for step in steps:
            go(sample, step).wait_recv()
        project(join_rows(arrived, sample), tqkv_across)
        for at, part in enumerate(split_rows(attend(True), seq_count)):
            mixed_sent[sample, at] = part

        @pl.when(section < sections - 1)
        def _():
            for step in every:
                ahead(sample, step).start()

        @pl.when(section == sections - 1)
        def _():
            for step in steps:
                back(sample, step).start()
            returned[sample, me] = mixed_sent[sample, me]

    def finish(sample):
        @pl.when(sample == 0)
        def _():
            loads[4].wait()

        for step in steps:
            back(sample, step).wait_recv()
        mixed = join_rows(returned, sample)
        for low, high in chunks(width):
            y_out[sample, :, low:high] = (
                middle[sample, :, low:high]
                + factor(sample, 5, low, high)
                * jnp.dot(mixed, tout[:, low:high], preferred_element_type=jnp.float32)
            ).astype(jnp.bfloat16)

        store(sample).start()

    @pl.loop(0, samples + 2)
    def _(at):
        @pl.when(at < samples)
        def _():
            spatial(at)

        @pl.when((at == 0) & (section == 0))
        def _():
            turn(loads[3], tqkv, tqkv_across)

        @pl.when((at > 0) & (at <= samples))
        def _():
            temporal(at - 1)

        @pl.when((at < samples) & (section < sections - 1))
        def _():
            hop(at).start()

        @pl.when((at < samples) & (section > 0))
        def _():
            home(at).start()

        @pl.when((at > 1) & (section == sections - 1))
        def _():
            finish(at - 2)

    for sample in range(samples):
        for step in steps:
            go(sample, step).wait_send()

    @pl.when(section > 0)
    def _():
        for sample in range(samples):
            home(sample).wait_send()

    @pl.when(section < sections - 1)
    def _():
        loads[4].wait()
        for sample in range(samples):
            hop(sample).wait_send()
            for step in every:
                ahead(sample, step).wait_send()
            home(sample).wait_recv()
        for lend in lends:
            lend.wait_send()

    @pl.when(section == sections - 1)
    def _():
        for sample in range(samples):
            for step in steps:
                back(sample, step).wait_send()
            store(sample).wait()


def on_device(frames_in, spatial_qkv, spatial_out, temporal_qkv, temporal_out, modulation):
    samples, local_frames, patches, width = frames_in.shape
    assert local_frames == 1
    seq_count = lax.axis_size("seq")
    sections = lax.axis_size("section")
    head_width = spatial_out.shape[1]
    rows = patches // seq_count
    bf16, f32 = jnp.bfloat16, jnp.float32
    dma = pltpu.SemaphoreType.DMA
    anywhere = pl.BlockSpec(memory_space=pltpu.HBM)
    span = max(stop - start for start, stop, *_ in head_windows(head_width))
    hidden = pl.pallas_call(
        functools.partial(kernel, seq_count, sections),
        out_shape=jax.ShapeDtypeStruct((samples, patches, width), bf16),
        in_specs=[anywhere] * 6,
        out_specs=anywhere,
        scratch_shapes=[
            pltpu.VMEM(spatial_qkv.shape[:0:-1], bf16),
            pltpu.VMEM(spatial_out.shape[1:], bf16),
            pltpu.VMEM(temporal_qkv.shape[:0:-1], bf16),
            pltpu.VMEM(temporal_out.shape[1:], bf16),
            pltpu.VMEM((modulation.shape[2], samples, width), f32),
            pltpu.VMEM((samples, modulation.shape[2], width), f32),
            pltpu.VMEM(spatial_qkv.shape[1:], bf16),
            pltpu.VMEM(temporal_qkv.shape[1:], bf16),
            pltpu.VMEM(temporal_out.shape[1:], bf16),
            pltpu.VMEM((samples, width), f32),
            pltpu.VMEM((samples, 1, width), f32),
            pltpu.VMEM((samples, patches, width), bf16),
            pltpu.VMEM((samples, patches, width), bf16),
            pltpu.VMEM((samples, patches, width), bf16),
            pltpu.VMEM((patches, width), f32),
            pltpu.VMEM((samples, patches, width), f32),
            pltpu.VMEM((patches, 3 * head_width), f32),
            pltpu.VMEM((samples, seq_count, rows, width), bf16),
            pltpu.VMEM((samples, seq_count, rows, width), bf16),
            pltpu.VMEM((samples, seq_count, rows, head_width), bf16),
            pltpu.VMEM((samples, seq_count, rows, head_width), bf16),
            pltpu.VMEM((samples, seq_count, rows, head_width), bf16),
            pltpu.VMEM((HEADS // 2, 2 * patches, span), bf16),
            pltpu.VMEM((HEADS // 2, span, span), bf16),
            pltpu.VMEM((patches, 2 * patches), bf16),
            dma((5,)),
            dma((samples,)),
            dma((samples,)),
            dma((2,)),
            dma((2,)),
            dma((samples,)),
            dma((samples,)),
            dma((samples, seq_count)),
            dma((samples, seq_count)),
            dma((samples, seq_count)),
            dma((samples, seq_count)),
            dma((samples, seq_count)),
            dma((samples, seq_count)),
            dma((samples,)),
            dma((samples,)),
        ],
        compiler_params=pltpu.CompilerParams(
            collective_id=0, has_side_effects=True, vmem_limit_bytes=60 * 1024 * 1024
        ),
    )(
        frames_in.reshape(samples, patches, width),
        jnp.swapaxes(spatial_qkv, 1, 2), spatial_out,
        jnp.swapaxes(temporal_qkv, 1, 2), temporal_out,
        jnp.swapaxes(modulation, 1, 2),
    )
    return hidden.reshape(1, samples, 1, patches, width)


def solution(mesh):
    placed = (
        P(None, "seq", None, None),
        P("section", None, None),
        P("section", None, None),
        P("section", None, None),
        P("section", None, None),
        P("section", None, None, None),
    )
    return jax.shard_map(
        on_device,
        mesh=mesh,
        in_specs=placed,
        out_specs=P("section", None, "seq", None, None),
        check_vma=False,
    )
```

```python
import functools
import math

import jax
import jax.numpy as jnp
from jax import lax
from jax.experimental import pallas as pl
from jax.experimental.pallas import tpu as pltpu
from jax.sharding import PartitionSpec as P

HEADS = 8
LANES = 128
CHUNK = 256
MESH = pl.DeviceIdType.MESH


def chunks(width, size=CHUNK):
    return [(at, min(at + size, width)) for at in range(0, width, size)]


def head_windows(head_width):
    size = head_width // HEADS
    found = []
    for pair in range(HEADS // 2):
        low, high = 2 * pair * size, 2 * (pair + 1) * size
        start = low // LANES * LANES
        stop = min(head_width, -(-high // LANES) * LANES)
        found.append((start, stop, low, low + size, high))
    return found


def gather_windows(head_width, parts):
    columns = []
    for low, high in chunks(head_width, LANES):
        total = None
        for (start, stop), part in parts:
            if start <= low and high <= stop:
                piece = part[:, low - start : high - start]
                total = piece if total is None else total + piece
        columns.append(total)
    return jnp.concatenate(columns, axis=1)


def flipped(index, step, count):
    total, bit = 0, 1
    while bit < count:
        total = total + lax.rem(index // bit + step // bit, 2) * bit
        bit *= 2
    return total


def norm_modulate(residual, offset, scaling):
    centered = residual - jnp.mean(residual, axis=-1, keepdims=True)
    variance = jnp.mean(centered * centered, axis=-1, keepdims=True)
    return centered * lax.rsqrt(variance + 1e-06) * (1.0 + scaling) + offset


def split_rows(tensor, count):
    rows = tensor.shape[0] // count
    return [tensor[r * rows : (r + 1) * rows].astype(jnp.bfloat16) for r in range(count)]


def join_rows(ref, sample):
    _, count, rows, width = ref.shape
    if rows % 16 == 0:
        return ref[sample].reshape(count * rows, width)
    parts = [ref[sample, r].astype(jnp.float32) for r in range(count)]
    return jnp.concatenate(parts, axis=0).astype(jnp.bfloat16)


def kernel(
    seq_count, sections,
    frames_hbm, sqkv_hbm, sout_hbm, tqkv_hbm, tout_hbm, mod_hbm,
    hidden_hbm,
    sqkv, sout, tqkv, tout, mod, factors, sqkv_across, tqkv_across, tout_before, gate_before, gates,
    x_in, x_out, y_out, residual, middle, qkv, sent, arrived, mixed_sent, returned, handed,
    pair_mask, square_mask, patch_mask,
    load_sem, frame_sem, store_sem, lend_send, lend_recv,
    hop_send, hop_recv, go_send, go_recv, back_send, back_recv, ahead_send, ahead_recv,
    home_send, home_recv,
):
    samples, patches, width = x_in.shape
    head_width = sout.shape[0]
    head_size = head_width // HEADS
    windows = head_windows(head_width)
    section = lax.axis_index("section")
    me = lax.axis_index("seq")

    loads = [
        pltpu.make_async_copy(src.at[0], dst, load_sem.at[at])
        for at, (src, dst) in enumerate(
            ((mod_hbm, mod), (sqkv_hbm, sqkv), (sout_hbm, sout), (tqkv_hbm, tqkv), (tout_hbm, tout))
        )
    ]

    def frame_load(sample):
        return pltpu.make_async_copy(
            frames_hbm.at[sample], x_in.at[sample], frame_sem.at[sample]
        )

    @pl.when(section == 0)
    def _():
        frame_load(0).start()

    loads[0].start()
    loads[1].start()

    barrier = pltpu.get_barrier_semaphore()
    for step in range(1, seq_count):
        pl.semaphore_signal(
            barrier, inc=1, device_id={"seq": flipped(me, step, seq_count)}, device_id_type=MESH
        )
    def greet(step):
        for other in range(seq_count):
            pl.semaphore_signal(
                barrier, inc=1,
                device_id={"section": section + step, "seq": other}, device_id_type=MESH,
            )

    @pl.when(section > 0)
    def _():
        greet(-1)

    @pl.when(section < sections - 1)
    def _():
        greet(1)

    for at, (start, stop, low, center, high) in enumerate(windows):
        span = stop - start
        lane = lax.broadcasted_iota(jnp.int32, (2 * patches, span), 1) + start
        row = lax.broadcasted_iota(jnp.int32, (2 * patches, span), 0)
        first = jnp.where((lane >= low) & (lane < center), 1.0, 0.0)
        second = jnp.where((lane >= center) & (lane < high), 1.0, 0.0)
        pair_mask[at, :, :span] = jnp.where(row < patches, first, second).astype(jnp.bfloat16)
        lane = lax.broadcasted_iota(jnp.int32, (span, span), 1) + start
        row = lax.broadcasted_iota(jnp.int32, (span, span), 0) + start
        first = (lane >= low) & (lane < center) & (row >= low) & (row < center)
        second = (lane >= center) & (lane < high) & (row >= center) & (row < high)
        square_mask[at, :span, :span] = jnp.where(
            first, 1.0, jnp.where(second, 1.0, 0.0)
        ).astype(jnp.bfloat16)
    group = patches // seq_count
    row = lax.broadcasted_iota(jnp.int32, (patches, 2 * patches), 0)
    lane = lax.broadcasted_iota(jnp.int32, (patches, 2 * patches), 1)
    patch_mask[...] = jnp.where(
        lax.rem(row, group) == lax.rem(lane, group), 1.0, 0.0
    ).astype(jnp.bfloat16)

    def turn(load, stored, across):
        load.wait()
        for low, high in chunks(3 * head_width):
            across[:, low:high] = stored[low:high, :].T

    turn(loads[1], sqkv, sqkv_across)
    for load in loads[2:]:
        load.start()

    @pl.when(section == 0)
    def _():
        for sample in range(1, samples):
            frame_load(sample).start()

    beside = jnp.minimum(section, 1) + jnp.minimum(sections - 1 - section, 1)
    pl.semaphore_wait(barrier, seq_count - 1 + seq_count * beside)

    def following(seq=None):
        place = {"section": lax.rem(section + 1, sections)}
        if seq is not None:
            place["seq"] = seq
        return place

    lends = [
        pltpu.make_async_remote_copy(
            src_ref=src, dst_ref=dst, send_sem=lend_send.at[at], recv_sem=lend_recv.at[at],
            device_id=following(), device_id_type=MESH,
        )
        for at, (src, dst) in enumerate(
            ((tout_hbm.at[0], tout_before), (mod_hbm.at[0, mod.shape[0] - 1], gate_before))
        )
    ]

    @pl.when(section < sections - 1)
    def _():
        for lend in lends:
            lend.start()

    @pl.when(section > 0)
    def _():
        turn(loads[3], tqkv, tqkv_across)

    def factor(sample, row, low=0, high=width):
        return factors[sample, row : row + 1, low:high]

    def project(rows, across):
        for low, high in chunks(3 * head_width):
            qkv[:, low:high] = jnp.dot(
                rows, across[:, low:high], preferred_element_type=jnp.float32
            )

    def attend(same_patch):
        queries = qkv[:, :head_width]
        aligned = head_width // LANES * LANES
        lookups = qkv[:, aligned : 2 * head_width]
        if aligned != head_width:
            reach = 2 * head_width - aligned
            lookups = pltpu.roll(lookups, reach - (head_width - aligned), 1)[:, :head_width]
        values = qkv[:, 2 * head_width :].astype(jnp.bfloat16)
        squares = jnp.concatenate([queries * queries, lookups * lookups], axis=0)
        squares = squares.astype(jnp.bfloat16)
        parts = []
        for at, (start, stop, *_) in enumerate(windows):
            span = stop - start
            parts.append(((start, stop), jnp.dot(
                squares[:, start:stop], square_mask[at, :span, :span],
                preferred_element_type=jnp.float32,
            )))
        norms = lax.rsqrt(gather_windows(head_width, parts) * (1.0 / head_size) + 1e-06)
        scale = math.log2(math.e) / math.sqrt(head_size)
        queries = (queries * (norms[:patches] * scale)).astype(jnp.bfloat16)
        lookups = (lookups * norms[patches:]).astype(jnp.bfloat16)
        exponents = []
        for at, (start, stop, *_) in enumerate(windows):
            part = lookups[:, start:stop]
            both = jnp.concatenate([part, part], axis=0) * pair_mask[at, :, : stop - start]
            exponents.append(lax.dot_general(
                queries[:, start:stop], both, (((1,), (1,)), ((), ())),
                preferred_element_type=jnp.float32,
            ))
        exponents = [jnp.exp2(scores).astype(jnp.bfloat16) for scores in exponents]
        if same_patch:
            exponents = [exponent * patch_mask[...] for exponent in exponents]
        tops, bottoms = [], []
        for at, (start, stop, *_) in enumerate(windows):
            mask = pair_mask[at, :, : stop - start]
            part = values[:, start:stop]
            both = jnp.concatenate([part, part], axis=0) * mask
            bottoms.append(((start, stop), jnp.dot(
                exponents[at], mask, preferred_element_type=jnp.float32
            )))
            tops.append(((start, stop), jnp.dot(
                exponents[at], both, preferred_element_type=jnp.float32
            )))
        return gather_windows(head_width, tops) / gather_windows(head_width, bottoms)

    def exchange(source, target, send_sem, recv_sem, sample, step):
        peer = flipped(me, step, seq_count)
        return pltpu.make_async_remote_copy(
            src_ref=source.at[sample, peer],
            dst_ref=target.at[sample, me],
            send_sem=send_sem.at[sample, step],
            recv_sem=recv_sem.at[sample, step],
            device_id={"seq": peer},
            device_id_type=MESH,
        )

    def go(sample, step):
        return exchange(sent, arrived, go_send, go_recv, sample, step)

    def back(sample, step):
        return exchange(mixed_sent, returned, back_send, back_recv, sample, step)

    def hop(sample):
        return pltpu.make_async_remote_copy(
            src_ref=y_out.at[sample],
            dst_ref=x_in.at[sample],
            send_sem=hop_send.at[sample],
            recv_sem=hop_recv.at[sample],
            device_id=following(),
            device_id_type=MESH,
        )

    def ahead(sample, step):
        peer = flipped(me, step, seq_count)
        return pltpu.make_async_remote_copy(
            src_ref=mixed_sent.at[sample, peer],
            dst_ref=handed.at[sample, me],
            send_sem=ahead_send.at[sample, step],
            recv_sem=ahead_recv.at[sample, step],
            device_id=following(peer),
            device_id_type=MESH,
        )

    def home(sample):
        return pltpu.make_async_remote_copy(
            src_ref=x_out.at[sample],
            dst_ref=hidden_hbm.at[sample],
            send_sem=home_send.at[sample],
            recv_sem=home_recv.at[sample],
            device_id={"section": lax.rem(section + sections - 1, sections)},
            device_id_type=MESH,
        )

    def store(sample):
        return pltpu.make_async_copy(
            y_out.at[sample], hidden_hbm.at[sample], store_sem.at[sample]
        )

    steps = range(seq_count - 1, 0, -1)
    every = range(seq_count - 1, -1, -1)

    def spatial(sample):
        @pl.when(sample == 0)
        def _():
            loads[0].wait()
            for video in range(samples):
                for row in range(mod.shape[0]):
                    factors[video, row : row + 1, :] = mod[row, video : video + 1, :]

        @pl.when(section == 0)
        def _():
            frame_load(sample).wait()
            residual[...] = x_in[sample].astype(jnp.float32)

        @pl.when(section > 0)
        def _():
            @pl.when(sample == 0)
            def _():
                for lend in lends:
                    lend.wait_recv()
                for video in range(samples):
                    gates[video] = gate_before[video : video + 1, :]

            hop(sample).wait_recv()
            for step in every:
                ahead(sample, step).wait_recv()
            mixed = join_rows(handed, sample)
            for low, high in chunks(width):
                residual[:, low:high] = x_in[sample, :, low:high].astype(jnp.float32) + gates[
                    sample, :, low:high
                ] * jnp.dot(mixed, tout_before[:, low:high], preferred_element_type=jnp.float32)

        normed = norm_modulate(residual[...], factor(sample, 0), factor(sample, 1))
        project(normed.astype(jnp.bfloat16), sqkv_across)
        mixed = attend(False).astype(jnp.bfloat16)

        @pl.when(sample == 0)
        def _():
            loads[2].wait()

        for low, high in chunks(width):
            middle[sample, :, low:high] = residual[:, low:high] + factor(
                sample, 2, low, high
            ) * jnp.dot(mixed, sout[:, low:high], preferred_element_type=jnp.float32)
        payload = norm_modulate(middle[sample], factor(sample, 3), factor(sample, 4))
        for at, part in enumerate(split_rows(payload, seq_count)):
            sent[sample, at] = part
        for step in steps:
            go(sample, step).start()
        arrived[sample, me] = sent[sample, me]
        y_out[sample] = middle[sample].astype(jnp.bfloat16)

        @pl.when(section > 0)
        def _():
            x_out[sample] = residual[...].astype(jnp.bfloat16)

    def temporal(sample):
        for step in steps:
            go(sample, step).wait_recv()
        project(join_rows(arrived, sample), tqkv_across)
        for at, part in enumerate(split_rows(attend(True), seq_count)):
            mixed_sent[sample, at] = part

        @pl.when(section < sections - 1)
        def _():
            for step in every:
                ahead(sample, step).start()

        @pl.when(section == sections - 1)
        def _():
            for step in steps:
                back(sample, step).start()
            returned[sample, me] = mixed_sent[sample, me]

    def finish(sample):
        @pl.when(sample == 0)
        def _():
            loads[4].wait()

        for step in steps:
            back(sample, step).wait_recv()
        mixed = join_rows(returned, sample)
        for low, high in chunks(width):
            y_out[sample, :, low:high] = (
                middle[sample, :, low:high]
                + factor(sample, 5, low, high)
                * jnp.dot(mixed, tout[:, low:high], preferred_element_type=jnp.float32)
            ).astype(jnp.bfloat16)

        store(sample).start()

    @pl.loop(0, samples + 2)
    def _(at):
        @pl.when(at < samples)
        def _():
            spatial(at)

        @pl.when((at == 0) & (section == 0))
        def _():
            turn(loads[3], tqkv, tqkv_across)

        @pl.when((at > 0) & (at <= samples))
        def _():
            temporal(at - 1)

        @pl.when((at < samples) & (section < sections - 1))
        def _():
            hop(at).start()

        @pl.when((at < samples) & (section > 0))
        def _():
            home(at).start()

        @pl.when((at > 1) & (section == sections - 1))
        def _():
            finish(at - 2)

    for sample in range(samples):
        for step in steps:
            go(sample, step).wait_send()

    @pl.when(section > 0)
    def _():
        for sample in range(samples):
            home(sample).wait_send()

    @pl.when(section < sections - 1)
    def _():
        loads[4].wait()
        for sample in range(samples):
            hop(sample).wait_send()
            for step in every:
                ahead(sample, step).wait_send()
            home(sample).wait_recv()
        for lend in lends:
            lend.wait_send()

    @pl.when(section == sections - 1)
    def _():
        for sample in range(samples):
            for step in steps:
                back(sample, step).wait_send()
            store(sample).wait()


def on_device(frames_in, spatial_qkv, spatial_out, temporal_qkv, temporal_out, modulation):
    samples, local_frames, patches, width = frames_in.shape
    assert local_frames == 1
    seq_count = lax.axis_size("seq")
    sections = lax.axis_size("section")
    head_width = spatial_out.shape[1]
    rows = patches // seq_count
    bf16, f32 = jnp.bfloat16, jnp.float32
    dma = pltpu.SemaphoreType.DMA
    anywhere = pl.BlockSpec(memory_space=pltpu.HBM)
    span = max(stop - start for start, stop, *_ in head_windows(head_width))
    hidden = pl.pallas_call(
        functools.partial(kernel, seq_count, sections),
        out_shape=jax.ShapeDtypeStruct((samples, patches, width), bf16),
        in_specs=[anywhere] * 6,
        out_specs=anywhere,
        scratch_shapes=[
            pltpu.VMEM(spatial_qkv.shape[:0:-1], bf16),
            pltpu.VMEM(spatial_out.shape[1:], bf16),
            pltpu.VMEM(temporal_qkv.shape[:0:-1], bf16),
            pltpu.VMEM(temporal_out.shape[1:], bf16),
            pltpu.VMEM((modulation.shape[2], samples, width), f32),
            pltpu.VMEM((samples, modulation.shape[2], width), f32),
            pltpu.VMEM(spatial_qkv.shape[1:], bf16),
            pltpu.VMEM(temporal_qkv.shape[1:], bf16),
            pltpu.VMEM(temporal_out.shape[1:], bf16),
            pltpu.VMEM((samples, width), f32),
            pltpu.VMEM((samples, 1, width), f32),
            pltpu.VMEM((samples, patches, width), bf16),
            pltpu.VMEM((samples, patches, width), bf16),
            pltpu.VMEM((samples, patches, width), bf16),
            pltpu.VMEM((patches, width), f32),
            pltpu.VMEM((samples, patches, width), f32),
            pltpu.VMEM((patches, 3 * head_width), f32),
            pltpu.VMEM((samples, seq_count, rows, width), bf16),
            pltpu.VMEM((samples, seq_count, rows, width), bf16),
            pltpu.VMEM((samples, seq_count, rows, head_width), bf16),
            pltpu.VMEM((samples, seq_count, rows, head_width), bf16),
            pltpu.VMEM((samples, seq_count, rows, head_width), bf16),
            pltpu.VMEM((HEADS // 2, 2 * patches, span), bf16),
            pltpu.VMEM((HEADS // 2, span, span), bf16),
            pltpu.VMEM((patches, 2 * patches), bf16),
            dma((5,)),
            dma((samples,)),
            dma((samples,)),
            dma((2,)),
            dma((2,)),
            dma((samples,)),
            dma((samples,)),
            dma((samples, seq_count)),
            dma((samples, seq_count)),
            dma((samples, seq_count)),
            dma((samples, seq_count)),
            dma((samples, seq_count)),
            dma((samples, seq_count)),
            dma((samples,)),
            dma((samples,)),
        ],
        compiler_params=pltpu.CompilerParams(
            collective_id=0, has_side_effects=True, vmem_limit_bytes=60 * 1024 * 1024
        ),
    )(
        frames_in.reshape(samples, patches, width),
        jnp.swapaxes(spatial_qkv, 1, 2), spatial_out,
        jnp.swapaxes(temporal_qkv, 1, 2), temporal_out,
        jnp.swapaxes(modulation, 1, 2),
    )
    return hidden.reshape(1, samples, 1, patches, width)


def solution(mesh):
    placed = (
        P(None, "seq", None, None),
        P("section", None, None),
        P("section", None, None),
        P("section", None, None),
        P("section", None, None),
        P("section", None, None, None),
    )
    return jax.shard_map(
        on_device,
        mesh=mesh,
        in_specs=placed,
        out_specs=P("section", None, "seq", None, None),
        check_vma=False,
    )
```

```python
import functools
import math

import jax
import jax.numpy as jnp
from jax import lax
from jax.experimental import pallas as pl
from jax.experimental.pallas import tpu as pltpu
from jax.sharding import PartitionSpec as P

HEADS = 8
LANES = 128
CHUNK = 256
MESH = pl.DeviceIdType.MESH


def chunks(width, size=CHUNK):
    return [(at, min(at + size, width)) for at in range(0, width, size)]


def head_windows(head_width):
    size = head_width // HEADS
    found = []
    for pair in range(HEADS // 2):
        low, high = 2 * pair * size, 2 * (pair + 1) * size
        start = low // LANES * LANES
        stop = min(head_width, -(-high // LANES) * LANES)
        found.append((start, stop, low, low + size, high))
    return found


def gather_windows(head_width, parts):
    columns = []
    for low, high in chunks(head_width, LANES):
        total = None
        for (start, stop), part in parts:
            if start <= low and high <= stop:
                piece = part[:, low - start : high - start]
                total = piece if total is None else total + piece
        columns.append(total)
    return jnp.concatenate(columns, axis=1)


def flipped(index, step, count):
    total, bit = 0, 1
    while bit < count:
        total = total + lax.rem(index // bit + step // bit, 2) * bit
        bit *= 2
    return total


def norm_modulate(residual, offset, scaling):
    near = residual - jnp.mean(residual[:, :CHUNK], axis=-1, keepdims=True)
    rest = jnp.mean(near, axis=-1, keepdims=True)
    variance = jnp.mean(near * near, axis=-1, keepdims=True) - rest * rest
    return (near - rest) * lax.rsqrt(variance + 1e-06) * (1.0 + scaling) + offset


def split_rows(tensor, count):
    rows = tensor.shape[0] // count
    return [tensor[r * rows : (r + 1) * rows].astype(jnp.bfloat16) for r in range(count)]


def join_rows(ref, sample):
    _, count, rows, width = ref.shape
    if rows % 16 == 0:
        return ref[sample].reshape(count * rows, width)
    parts = [ref[sample, r].astype(jnp.float32) for r in range(count)]
    return jnp.concatenate(parts, axis=0).astype(jnp.bfloat16)


def kernel(
    seq_count, sections,
    frames_hbm, sqkv_hbm, sout_hbm, tqkv_hbm, tout_hbm, mod_hbm,
    hidden_hbm,
    sqkv, sout, tqkv, tout, mod, factors, sqkv_across, tqkv_across, tout_before, gate_before, gates,
    x_in, x_out, y_out, residual, middle, qkv, sent, arrived, mixed_sent, returned, handed,
    pair_mask, square_mask, patch_mask,
    load_sem, first_sem, frame_sem, store_sem, lend_send, lend_recv,
    hop_send, hop_recv, go_send, go_recv, back_send, back_recv, ahead_send, ahead_recv,
    home_send, home_recv,
):
    samples, patches, width = x_in.shape
    head_width = sout.shape[0]
    head_size = head_width // HEADS
    windows = head_windows(head_width)
    section = lax.axis_index("section")
    me = lax.axis_index("seq")
    peers = [flipped(me, step, seq_count) for step in range(seq_count)]
    after = lax.rem(section + 1, sections)
    before = lax.rem(section + sections - 1, sections)

    loads = [
        pltpu.make_async_copy(src.at[0], dst, load_sem.at[at])
        for at, (src, dst) in enumerate(
            ((mod_hbm, mod), (sout_hbm, sout), (tqkv_hbm, tqkv), (tout_hbm, tout))
        )
    ]

    def frame_load(sample):
        return pltpu.make_async_copy(
            frames_hbm.at[sample], x_in.at[sample], frame_sem.at[sample]
        )

    @pl.when(section == 0)
    def _():
        frame_load(0).start()

    first_loads = [
        pltpu.make_async_copy(
            sqkv_hbm.at[0, pl.ds(low, high - low)], sqkv.at[pl.ds(low, high - low)], first_sem.at[at]
        )
        for at, (low, high) in enumerate(chunks(3 * head_width))
    ]
    loads[0].start()
    for load in first_loads:
        load.start()
    loads[1].start()

    barrier = pltpu.get_barrier_semaphore()
    for step in range(1, seq_count):
        pl.semaphore_signal(
            barrier, inc=1, device_id={"seq": peers[step]}, device_id_type=MESH
        )
    def greet(step):
        for other in range(seq_count):
            pl.semaphore_signal(
                barrier, inc=1,
                device_id={"section": section + step, "seq": other}, device_id_type=MESH,
            )

    @pl.when(section > 0)
    def _():
        greet(-1)

    @pl.when(section < sections - 1)
    def _():
        greet(1)

    for at, (start, stop, low, center, high) in enumerate(windows):
        span = stop - start
        lane = lax.broadcasted_iota(jnp.int32, (2 * patches, span), 1) + start
        row = lax.broadcasted_iota(jnp.int32, (2 * patches, span), 0)
        first = jnp.where((lane >= low) & (lane < center), 1.0, 0.0)
        second = jnp.where((lane >= center) & (lane < high), 1.0, 0.0)
        pair_mask[at, :, :span] = jnp.where(row < patches, first, second).astype(jnp.bfloat16)
        lane = lax.broadcasted_iota(jnp.int32, (span, span), 1) + start
        row = lax.broadcasted_iota(jnp.int32, (span, span), 0) + start
        first = (lane >= low) & (lane < center) & (row >= low) & (row < center)
        second = (lane >= center) & (lane < high) & (row >= center) & (row < high)
        square_mask[at, :span, :span] = jnp.where(
            first, 1.0, jnp.where(second, 1.0, 0.0)
        ).astype(jnp.bfloat16)
    group = patches // seq_count
    row = lax.broadcasted_iota(jnp.int32, (patches, 2 * patches), 0)
    lane = lax.broadcasted_iota(jnp.int32, (patches, 2 * patches), 1)
    patch_mask[...] = jnp.where(
        lax.rem(row, group) == lax.rem(lane, group), 1.0, 0.0
    ).astype(jnp.bfloat16)

    def turn(load, stored, across):
        load.wait()
        for low, high in chunks(3 * head_width):
            across[:, low:high] = stored[low:high, :].T

    @pl.when(section == 0)
    def _():
        tout_before[...] = jnp.zeros_like(tout_before)
        handed[...] = jnp.zeros_like(handed)
        gates[...] = jnp.zeros_like(gates)

    for load, (low, high) in zip(first_loads, chunks(3 * head_width)):
        load.wait()
        sqkv_across[:, low:high] = sqkv[low:high, :].T
    for load in loads[2:]:
        load.start()

    @pl.when(section == 0)
    def _():
        for sample in range(1, samples):
            frame_load(sample).start()

    beside = jnp.minimum(section, 1) + jnp.minimum(sections - 1 - section, 1)
    pl.semaphore_wait(barrier, seq_count - 1 + seq_count * beside)

    def following(seq=None):
        place = {"section": after}
        if seq is not None:
            place["seq"] = seq
        return place

    lends = [
        pltpu.make_async_remote_copy(
            src_ref=src, dst_ref=dst, send_sem=lend_send.at[at], recv_sem=lend_recv.at[at],
            device_id=following(), device_id_type=MESH,
        )
        for at, (src, dst) in enumerate(
            ((tout_hbm.at[0], tout_before), (mod_hbm.at[0, mod.shape[0] - 1], gate_before))
        )
    ]

    @pl.when(section < sections - 1)
    def _():
        for lend in lends:
            lend.start()

    @pl.when(section > 0)
    def _():
        turn(loads[2], tqkv, tqkv_across)

    def factor(sample, row, low=0, high=width):
        return factors[sample, row : row + 1, low:high]

    def project(rows, across):
        for low, high in chunks(3 * head_width):
            qkv[:, low:high] = jnp.dot(
                rows, across[:, low:high], preferred_element_type=jnp.float32
            )

    def attend(same_patch):
        queries = qkv[:, :head_width]
        aligned = head_width // LANES * LANES
        lookups = qkv[:, aligned : 2 * head_width]
        if aligned != head_width:
            reach = 2 * head_width - aligned
            lookups = pltpu.roll(lookups, reach - (head_width - aligned), 1)[:, :head_width]
        values = qkv[:, 2 * head_width :].astype(jnp.bfloat16)
        squares = jnp.concatenate([queries * queries, lookups * lookups], axis=0)
        squares = squares.astype(jnp.bfloat16)
        parts = []
        for at, (start, stop, *_) in enumerate(windows):
            span = stop - start
            parts.append(((start, stop), jnp.dot(
                squares[:, start:stop], square_mask[at, :span, :span],
                preferred_element_type=jnp.float32,
            )))
        norms = lax.rsqrt(gather_windows(head_width, parts) * (1.0 / head_size) + 1e-06)
        scale = math.log2(math.e) / math.sqrt(head_size)
        queries = (queries * (norms[:patches] * scale)).astype(jnp.bfloat16)
        lookups = (lookups * norms[patches:]).astype(jnp.bfloat16)
        exponents = []
        for at, (start, stop, *_) in enumerate(windows):
            part = lookups[:, start:stop]
            both = jnp.concatenate([part, part], axis=0) * pair_mask[at, :, : stop - start]
            exponents.append(lax.dot_general(
                queries[:, start:stop], both, (((1,), (1,)), ((), ())),
                preferred_element_type=jnp.float32,
            ))
        exponents = [jnp.exp2(scores).astype(jnp.bfloat16) for scores in exponents]
        if same_patch:
            exponents = [exponent * patch_mask[...] for exponent in exponents]
        tops, bottoms = [], []
        for at, (start, stop, *_) in enumerate(windows):
            mask = pair_mask[at, :, : stop - start]
            part = values[:, start:stop]
            both = jnp.concatenate([part, part], axis=0) * mask
            bottoms.append(((start, stop), jnp.dot(
                exponents[at], mask, preferred_element_type=jnp.float32
            )))
            tops.append(((start, stop), jnp.dot(
                exponents[at], both, preferred_element_type=jnp.float32
            )))
        return gather_windows(head_width, tops) / gather_windows(head_width, bottoms)

    def exchange(source, target, send_sem, recv_sem, sample, step):
        peer = peers[step]
        return pltpu.make_async_remote_copy(
            src_ref=source.at[sample, peer],
            dst_ref=target.at[sample, me],
            send_sem=send_sem.at[sample, step],
            recv_sem=recv_sem.at[sample, step],
            device_id={"seq": peer},
            device_id_type=MESH,
        )

    def go(sample, step):
        return exchange(sent, arrived, go_send, go_recv, sample, step)

    def back(sample, step):
        return exchange(mixed_sent, returned, back_send, back_recv, sample, step)

    def hop(sample):
        return pltpu.make_async_remote_copy(
            src_ref=y_out.at[sample],
            dst_ref=x_in.at[sample],
            send_sem=hop_send.at[sample],
            recv_sem=hop_recv.at[sample],
            device_id=following(),
            device_id_type=MESH,
        )

    def ahead(sample, step):
        peer = peers[step]
        return pltpu.make_async_remote_copy(
            src_ref=mixed_sent.at[sample, peer],
            dst_ref=handed.at[sample, me],
            send_sem=ahead_send.at[sample, step],
            recv_sem=ahead_recv.at[sample, step],
            device_id=following(peer),
            device_id_type=MESH,
        )

    def home(sample):
        return pltpu.make_async_remote_copy(
            src_ref=x_out.at[sample],
            dst_ref=hidden_hbm.at[sample],
            send_sem=home_send.at[sample],
            recv_sem=home_recv.at[sample],
            device_id={"section": before},
            device_id_type=MESH,
        )

    def store(sample):
        return pltpu.make_async_copy(
            y_out.at[sample], hidden_hbm.at[sample], store_sem.at[sample]
        )

    steps = range(seq_count - 1, 0, -1)
    every = range(seq_count - 1, -1, -1)

    def spatial(sample):
        @pl.when(sample == 0)
        def _():
            loads[0].wait()
            loads[1].wait()
            for video in range(samples):
                for row in range(mod.shape[0]):
                    factors[video, row : row + 1, :] = mod[row, video : video + 1, :]

        @pl.when(section == 0)
        def _():
            frame_load(sample).wait()

        @pl.when(section > 0)
        def _():
            @pl.when(sample == 0)
            def _():
                for lend in lends:
                    lend.wait_recv()
                for video in range(samples):
                    gates[video] = gate_before[video : video + 1, :]

            hop(sample).wait_recv()
            for step in every:
                ahead(sample, step).wait_recv()

        mixed = join_rows(handed, sample)
        for low, high in chunks(width):
            residual[:, low:high] = x_in[sample, :, low:high].astype(jnp.float32) + gates[
                sample, :, low:high
            ] * jnp.dot(mixed, tout_before[:, low:high], preferred_element_type=jnp.float32)

        normed = norm_modulate(residual[...], factor(sample, 0), factor(sample, 1))
        project(normed.astype(jnp.bfloat16), sqkv_across)
        mixed = attend(False).astype(jnp.bfloat16)

        for low, high in chunks(width):
            middle[sample, :, low:high] = residual[:, low:high] + factor(
                sample, 2, low, high
            ) * jnp.dot(mixed, sout[:, low:high], preferred_element_type=jnp.float32)
        payload = norm_modulate(middle[sample], factor(sample, 3), factor(sample, 4))
        for at, part in enumerate(split_rows(payload, seq_count)):
            sent[sample, at] = part
        for step in steps:
            go(sample, step).start()
        arrived[sample, me] = sent[sample, me]
        y_out[sample] = middle[sample].astype(jnp.bfloat16)

        x_out[sample] = residual[...].astype(jnp.bfloat16)

    def temporal(sample):
        for step in steps:
            go(sample, step).wait_recv()
        project(join_rows(arrived, sample), tqkv_across)
        for at, part in enumerate(split_rows(attend(True), seq_count)):
            mixed_sent[sample, at] = part

        @pl.when(section < sections - 1)
        def _():
            for step in every:
                ahead(sample, step).start()

        @pl.when(section == sections - 1)
        def _():
            for step in steps:
                back(sample, step).start()
            returned[sample, me] = mixed_sent[sample, me]

    def finish(sample):
        @pl.when(sample == 0)
        def _():
            loads[3].wait()

        for step in steps:
            back(sample, step).wait_recv()
        mixed = join_rows(returned, sample)
        for low, high in chunks(width):
            y_out[sample, :, low:high] = (
                middle[sample, :, low:high]
                + factor(sample, 5, low, high)
                * jnp.dot(mixed, tout[:, low:high], preferred_element_type=jnp.float32)
            ).astype(jnp.bfloat16)

        store(sample).start()

    @pl.loop(0, samples + 2)
    def _(at):
        @pl.when(at < samples)
        def _():
            spatial(at)

        @pl.when((at == 0) & (section == 0))
        def _():
            turn(loads[2], tqkv, tqkv_across)

        @pl.when((at > 0) & (at <= samples))
        def _():
            temporal(at - 1)

        @pl.when((at < samples) & (section < sections - 1))
        def _():
            hop(at).start()

        @pl.when((at < samples) & (section > 0))
        def _():
            home(at).start()

        @pl.when((at > 1) & (section == sections - 1))
        def _():
            finish(at - 2)

    for sample in range(samples):
        for step in steps:
            go(sample, step).wait_send()

    @pl.when(section > 0)
    def _():
        for sample in range(samples):
            home(sample).wait_send()

    @pl.when(section < sections - 1)
    def _():
        loads[3].wait()
        for sample in range(samples):
            hop(sample).wait_send()
            for step in every:
                ahead(sample, step).wait_send()
            home(sample).wait_recv()
        for lend in lends:
            lend.wait_send()

    @pl.when(section == sections - 1)
    def _():
        for sample in range(samples):
            for step in steps:
                back(sample, step).wait_send()
            store(sample).wait()


def on_device(frames_in, spatial_qkv, spatial_out, temporal_qkv, temporal_out, modulation):
    samples, local_frames, patches, width = frames_in.shape
    assert local_frames == 1
    seq_count = lax.axis_size("seq")
    sections = lax.axis_size("section")
    head_width = spatial_out.shape[1]
    rows = patches // seq_count
    bf16, f32 = jnp.bfloat16, jnp.float32
    dma = pltpu.SemaphoreType.DMA
    anywhere = pl.BlockSpec(memory_space=pltpu.HBM)
    span = max(stop - start for start, stop, *_ in head_windows(head_width))
    hidden = pl.pallas_call(
        functools.partial(kernel, seq_count, sections),
        out_shape=jax.ShapeDtypeStruct((samples, patches, width), bf16),
        in_specs=[anywhere] * 6,
        out_specs=anywhere,
        scratch_shapes=[
            pltpu.VMEM(spatial_qkv.shape[:0:-1], bf16),
            pltpu.VMEM(spatial_out.shape[1:], bf16),
            pltpu.VMEM(temporal_qkv.shape[:0:-1], bf16),
            pltpu.VMEM(temporal_out.shape[1:], bf16),
            pltpu.VMEM((modulation.shape[2], samples, width), f32),
            pltpu.VMEM((samples, modulation.shape[2], width), f32),
            pltpu.VMEM(spatial_qkv.shape[1:], bf16),
            pltpu.VMEM(temporal_qkv.shape[1:], bf16),
            pltpu.VMEM(temporal_out.shape[1:], bf16),
            pltpu.VMEM((samples, width), f32),
            pltpu.VMEM((samples, 1, width), f32),
            pltpu.VMEM((samples, patches, width), bf16),
            pltpu.VMEM((samples, patches, width), bf16),
            pltpu.VMEM((samples, patches, width), bf16),
            pltpu.VMEM((patches, width), f32),
            pltpu.VMEM((samples, patches, width), f32),
            pltpu.VMEM((patches, 3 * head_width), f32),
            pltpu.VMEM((samples, seq_count, rows, width), bf16),
            pltpu.VMEM((samples, seq_count, rows, width), bf16),
            pltpu.VMEM((samples, seq_count, rows, head_width), bf16),
            pltpu.VMEM((samples, seq_count, rows, head_width), bf16),
            pltpu.VMEM((samples, seq_count, rows, head_width), bf16),
            pltpu.VMEM((HEADS // 2, 2 * patches, span), bf16),
            pltpu.VMEM((HEADS // 2, span, span), bf16),
            pltpu.VMEM((patches, 2 * patches), bf16),
            dma((4,)),
            dma((len(chunks(3 * head_width)),)),
            dma((samples,)),
            dma((samples,)),
            dma((2,)),
            dma((2,)),
            dma((samples,)),
            dma((samples,)),
            dma((samples, seq_count)),
            dma((samples, seq_count)),
            dma((samples, seq_count)),
            dma((samples, seq_count)),
            dma((samples, seq_count)),
            dma((samples, seq_count)),
            dma((samples,)),
            dma((samples,)),
        ],
        compiler_params=pltpu.CompilerParams(
            collective_id=0, has_side_effects=True, vmem_limit_bytes=60 * 1024 * 1024
        ),
    )(
        frames_in.reshape(samples, patches, width),
        jnp.swapaxes(spatial_qkv, 1, 2), spatial_out,
        jnp.swapaxes(temporal_qkv, 1, 2), temporal_out,
        jnp.swapaxes(modulation, 1, 2),
    )
    return hidden.reshape(1, samples, 1, patches, width)


def solution(mesh):
    placed = (
        P(None, "seq", None, None),
        P("section", None, None),
        P("section", None, None),
        P("section", None, None),
        P("section", None, None),
        P("section", None, None, None),
    )
    return jax.shard_map(
        on_device,
        mesh=mesh,
        in_specs=placed,
        out_specs=P("section", None, "seq", None, None),
        check_vma=False,
    )
```

```python
import functools
import math

import jax
import jax.numpy as jnp
from jax import lax
from jax.experimental import pallas as pl
from jax.experimental.pallas import tpu as pltpu
from jax.sharding import PartitionSpec as P

HEADS = 8
LANES = 128
CHUNK = 256
MESH = pl.DeviceIdType.MESH


def chunks(width, size=CHUNK):
    return [(at, min(at + size, width)) for at in range(0, width, size)]


def head_windows(head_width):
    size = head_width // HEADS
    found = []
    for pair in range(HEADS // 2):
        low, high = 2 * pair * size, 2 * (pair + 1) * size
        start = low // LANES * LANES
        stop = min(head_width, -(-high // LANES) * LANES)
        found.append((start, stop, low, low + size, high))
    return found


def gather_windows(head_width, parts):
    columns = []
    for low, high in chunks(head_width, LANES):
        total = None
        for (start, stop), part in parts:
            if start <= low and high <= stop:
                piece = part[:, low - start : high - start]
                total = piece if total is None else total + piece
        columns.append(total)
    return jnp.concatenate(columns, axis=1)


def flipped(index, step, count):
    total, bit = 0, 1
    while bit < count:
        total = total + lax.rem(index // bit + step // bit, 2) * bit
        bit *= 2
    return total


def norm_modulate(residual, offset, scaling):
    near = residual - jnp.mean(residual[:, :CHUNK], axis=-1, keepdims=True)
    rest = jnp.mean(near, axis=-1, keepdims=True)
    variance = jnp.mean(near * near, axis=-1, keepdims=True) - rest * rest
    return (near - rest) * lax.rsqrt(variance + 1e-06) * (1.0 + scaling) + offset


def split_rows(tensor, count):
    rows = tensor.shape[0] // count
    return [tensor[r * rows : (r + 1) * rows].astype(jnp.bfloat16) for r in range(count)]


def join_rows(ref, sample):
    _, count, rows, width = ref.shape
    if rows % 16 == 0:
        return ref[sample].reshape(count * rows, width)
    parts = [ref[sample, r].astype(jnp.float32) for r in range(count)]
    return jnp.concatenate(parts, axis=0).astype(jnp.bfloat16)


def kernel(
    seq_count, sections,
    frames_hbm, sqkv_hbm, sout_hbm, tqkv_hbm, tout_hbm, mod_hbm,
    hidden_hbm,
    sqkv, sout, tqkv, tout, mod, factors, sqkv_across, tqkv_across, tout_before, gate_before, gates,
    x_in, x_out, y_out, residual, middle, qkv, sent, arrived, mixed_sent, returned, handed,
    pair_mask, square_mask, patch_mask,
    load_sem, first_sem, frame_sem, store_sem, lend_send, lend_recv,
    hop_send, hop_recv, go_send, go_recv, back_send, back_recv, ahead_send, ahead_recv,
    home_send, home_recv,
):
    samples, patches, width = x_in.shape
    head_width = sout.shape[0]
    head_size = head_width // HEADS
    windows = head_windows(head_width)
    section = lax.axis_index("section")
    me = lax.axis_index("seq")
    peers = [flipped(me, step, seq_count) for step in range(seq_count)]
    after = lax.rem(section + 1, sections)
    before = lax.rem(section + sections - 1, sections)

    loads = [
        pltpu.make_async_copy(src.at[0], dst, load_sem.at[at])
        for at, (src, dst) in enumerate(
            ((mod_hbm, mod), (sout_hbm, sout), (tqkv_hbm, tqkv), (tout_hbm, tout))
        )
    ]

    def frame_load(sample):
        return pltpu.make_async_copy(
            frames_hbm.at[sample], x_in.at[sample], frame_sem.at[sample]
        )

    @pl.when(section == 0)
    def _():
        frame_load(0).start()

    first_loads = [
        pltpu.make_async_copy(
            sqkv_hbm.at[0, pl.ds(low, high - low)], sqkv.at[pl.ds(low, high - low)], first_sem.at[at]
        )
        for at, (low, high) in enumerate(chunks(3 * head_width))
    ]
    loads[0].start()
    for load in first_loads:
        load.start()
    loads[1].start()

    barrier = pltpu.get_barrier_semaphore()
    for step in range(1, seq_count):
        pl.semaphore_signal(
            barrier, inc=1, device_id={"seq": peers[step]}, device_id_type=MESH
        )
    def greet(step):
        for other in range(seq_count):
            pl.semaphore_signal(
                barrier, inc=1,
                device_id={"section": section + step, "seq": other}, device_id_type=MESH,
            )

    @pl.when(section > 0)
    def _():
        greet(-1)

    @pl.when(section < sections - 1)
    def _():
        greet(1)

    for at, (start, stop, low, center, high) in enumerate(windows):
        span = stop - start
        lane = lax.broadcasted_iota(jnp.int32, (2 * patches, span), 1) + start
        row = lax.broadcasted_iota(jnp.int32, (2 * patches, span), 0)
        first = jnp.where((lane >= low) & (lane < center), 1.0, 0.0)
        second = jnp.where((lane >= center) & (lane < high), 1.0, 0.0)
        pair_mask[at, :, :span] = jnp.where(row < patches, first, second).astype(jnp.bfloat16)
        lane = lax.broadcasted_iota(jnp.int32, (span, span), 1) + start
        row = lax.broadcasted_iota(jnp.int32, (span, span), 0) + start
        first = (lane >= low) & (lane < center) & (row >= low) & (row < center)
        second = (lane >= center) & (lane < high) & (row >= center) & (row < high)
        square_mask[at, :span, :span] = jnp.where(
            first, 1.0, jnp.where(second, 1.0, 0.0)
        ).astype(jnp.bfloat16)
    group = patches // seq_count
    row = lax.broadcasted_iota(jnp.int32, (patches, 2 * patches), 0)
    lane = lax.broadcasted_iota(jnp.int32, (patches, 2 * patches), 1)
    patch_mask[...] = jnp.where(
        lax.rem(row, group) == lax.rem(lane, group), 1.0, 0.0
    ).astype(jnp.bfloat16)

    def turn(load, stored, across):
        load.wait()
        for low, high in chunks(3 * head_width):
            across[:, low:high] = stored[low:high, :].T

    @pl.when(section == 0)
    def _():
        tout_before[...] = jnp.zeros_like(tout_before)
        handed[...] = jnp.zeros_like(handed)
        gates[...] = jnp.zeros_like(gates)

    for load, (low, high) in zip(first_loads, chunks(3 * head_width)):
        load.wait()
        sqkv_across[:, low:high] = sqkv[low:high, :].T
    for load in loads[2:]:
        load.start()

    @pl.when(section == 0)
    def _():
        for sample in range(1, samples):
            frame_load(sample).start()

    beside = jnp.minimum(section, 1) + jnp.minimum(sections - 1 - section, 1)
    pl.semaphore_wait(barrier, seq_count - 1 + seq_count * beside)

    def following(seq=None):
        place = {"section": after}
        if seq is not None:
            place["seq"] = seq
        return place

    lends = [
        pltpu.make_async_remote_copy(
            src_ref=src, dst_ref=dst, send_sem=lend_send.at[at], recv_sem=lend_recv.at[at],
            device_id=following(), device_id_type=MESH,
        )
        for at, (src, dst) in enumerate(
            ((tout_hbm.at[0], tout_before), (mod_hbm.at[0, mod.shape[0] - 1], gate_before))
        )
    ]

    @pl.when(section < sections - 1)
    def _():
        for lend in lends:
            lend.start()

    @pl.when(section > 0)
    def _():
        turn(loads[2], tqkv, tqkv_across)

    def factor(sample, row, low=0, high=width):
        return factors[sample, row : row + 1, low:high]

    def project(rows, across):
        blocks = chunks(3 * head_width)
        keys = [b for b in blocks if b[1] > head_width and b[0] < 2 * head_width]
        for low, high in keys + [b for b in blocks if b not in keys]:
            qkv[:, low:high] = jnp.dot(
                rows, across[:, low:high], preferred_element_type=jnp.float32
            )

    def head_norms(tensor):
        squares = (tensor * tensor).astype(jnp.bfloat16)
        parts = []
        for at, (start, stop, *_) in enumerate(windows):
            span = stop - start
            parts.append(((start, stop), jnp.dot(
                squares[:, start:stop], square_mask[at, :span, :span],
                preferred_element_type=jnp.float32,
            )))
        return lax.rsqrt(gather_windows(head_width, parts) * (1.0 / head_size) + 1e-06)

    def attend(same_patch):
        queries = qkv[:, :head_width]
        aligned = head_width // LANES * LANES
        lookups = qkv[:, aligned : 2 * head_width]
        if aligned != head_width:
            reach = 2 * head_width - aligned
            lookups = pltpu.roll(lookups, reach - (head_width - aligned), 1)[:, :head_width]
        values = qkv[:, 2 * head_width :].astype(jnp.bfloat16)
        lookups = (lookups * head_norms(lookups)).astype(jnp.bfloat16)
        scale = math.log2(math.e) / math.sqrt(head_size)
        queries = (queries * (head_norms(queries) * scale)).astype(jnp.bfloat16)
        exponents = []
        for at, (start, stop, *_) in enumerate(windows):
            part = lookups[:, start:stop]
            both = jnp.concatenate([part, part], axis=0) * pair_mask[at, :, : stop - start]
            exponents.append(lax.dot_general(
                queries[:, start:stop], both, (((1,), (1,)), ((), ())),
                preferred_element_type=jnp.float32,
            ))
        exponents = [jnp.exp2(scores).astype(jnp.bfloat16) for scores in exponents]
        if same_patch:
            exponents = [exponent * patch_mask[...] for exponent in exponents]
        tops, bottoms = [], []
        for at, (start, stop, *_) in enumerate(windows):
            mask = pair_mask[at, :, : stop - start]
            part = values[:, start:stop]
            both = jnp.concatenate([part, part], axis=0) * mask
            bottoms.append(((start, stop), jnp.dot(
                exponents[at], mask, preferred_element_type=jnp.float32
            )))
            tops.append(((start, stop), jnp.dot(
                exponents[at], both, preferred_element_type=jnp.float32
            )))
        return gather_windows(head_width, tops) / gather_windows(head_width, bottoms)

    def exchange(source, target, send_sem, recv_sem, sample, step):
        peer = peers[step]
        return pltpu.make_async_remote_copy(
            src_ref=source.at[sample, peer],
            dst_ref=target.at[sample, me],
            send_sem=send_sem.at[sample, step],
            recv_sem=recv_sem.at[sample, step],
            device_id={"seq": peer},
            device_id_type=MESH,
        )

    def go(sample, step):
        return exchange(sent, arrived, go_send, go_recv, sample, step)

    def back(sample, step):
        return exchange(mixed_sent, returned, back_send, back_recv, sample, step)

    def hop(sample):
        return pltpu.make_async_remote_copy(
            src_ref=y_out.at[sample],
            dst_ref=x_in.at[sample],
            send_sem=hop_send.at[sample],
            recv_sem=hop_recv.at[sample],
            device_id=following(),
            device_id_type=MESH,
        )

    def ahead(sample, step):
        peer = peers[step]
        return pltpu.make_async_remote_copy(
            src_ref=mixed_sent.at[sample, peer],
            dst_ref=handed.at[sample, me],
            send_sem=ahead_send.at[sample, step],
            recv_sem=ahead_recv.at[sample, step],
            device_id=following(peer),
            device_id_type=MESH,
        )

    def home(sample):
        return pltpu.make_async_remote_copy(
            src_ref=x_out.at[sample],
            dst_ref=hidden_hbm.at[sample],
            send_sem=home_send.at[sample],
            recv_sem=home_recv.at[sample],
            device_id={"section": before},
            device_id_type=MESH,
        )

    def store(sample):
        return pltpu.make_async_copy(
            y_out.at[sample], hidden_hbm.at[sample], store_sem.at[sample]
        )

    steps = range(seq_count - 1, 0, -1)
    every = range(seq_count - 1, -1, -1)

    def spatial(sample):
        @pl.when(sample == 0)
        def _():
            loads[0].wait()
            loads[1].wait()
            for video in range(samples):
                for row in range(mod.shape[0]):
                    factors[video, row : row + 1, :] = mod[row, video : video + 1, :]

        @pl.when(section == 0)
        def _():
            frame_load(sample).wait()

        @pl.when(section > 0)
        def _():
            @pl.when(sample == 0)
            def _():
                for lend in lends:
                    lend.wait_recv()
                for video in range(samples):
                    gates[video] = gate_before[video : video + 1, :]

            hop(sample).wait_recv()
            for step in every:
                ahead(sample, step).wait_recv()

        mixed = join_rows(handed, sample)
        for low, high in chunks(width):
            residual[:, low:high] = x_in[sample, :, low:high].astype(jnp.float32) + gates[
                sample, :, low:high
            ] * jnp.dot(mixed, tout_before[:, low:high], preferred_element_type=jnp.float32)

        normed = norm_modulate(residual[...], factor(sample, 0), factor(sample, 1))
        project(normed.astype(jnp.bfloat16), sqkv_across)
        mixed = attend(False).astype(jnp.bfloat16)

        for low, high in chunks(width):
            middle[sample, :, low:high] = residual[:, low:high] + factor(
                sample, 2, low, high
            ) * jnp.dot(mixed, sout[:, low:high], preferred_element_type=jnp.float32)
        payload = norm_modulate(middle[sample], factor(sample, 3), factor(sample, 4))
        for at, part in enumerate(split_rows(payload, seq_count)):
            sent[sample, at] = part
        for step in steps:
            go(sample, step).start()
        arrived[sample, me] = sent[sample, me]
        y_out[sample] = middle[sample].astype(jnp.bfloat16)

        x_out[sample] = residual[...].astype(jnp.bfloat16)

    def temporal(sample):
        for step in steps:
            go(sample, step).wait_recv()
        project(join_rows(arrived, sample), tqkv_across)
        for at, part in enumerate(split_rows(attend(True), seq_count)):
            mixed_sent[sample, at] = part

        @pl.when(section < sections - 1)
        def _():
            for step in every:
                ahead(sample, step).start()

        @pl.when(section == sections - 1)
        def _():
            for step in steps:
                back(sample, step).start()
            returned[sample, me] = mixed_sent[sample, me]

    def finish(sample):
        @pl.when(sample == 0)
        def _():
            loads[3].wait()

        for step in steps:
            back(sample, step).wait_recv()
        mixed = join_rows(returned, sample)
        for low, high in chunks(width):
            y_out[sample, :, low:high] = (
                middle[sample, :, low:high]
                + factor(sample, 5, low, high)
                * jnp.dot(mixed, tout[:, low:high], preferred_element_type=jnp.float32)
            ).astype(jnp.bfloat16)

        store(sample).start()

    @pl.loop(0, samples + 2)
    def _(at):
        @pl.when(at < samples)
        def _():
            spatial(at)

        @pl.when((at == 0) & (section == 0))
        def _():
            turn(loads[2], tqkv, tqkv_across)

        @pl.when((at > 0) & (at <= samples))
        def _():
            temporal(at - 1)

        @pl.when((at < samples) & (section < sections - 1))
        def _():
            hop(at).start()

        @pl.when((at < samples) & (section > 0))
        def _():
            home(at).start()

        @pl.when((at > 1) & (section == sections - 1))
        def _():
            finish(at - 2)

    for sample in range(samples):
        for step in steps:
            go(sample, step).wait_send()

    @pl.when(section > 0)
    def _():
        for sample in range(samples):
            home(sample).wait_send()

    @pl.when(section < sections - 1)
    def _():
        loads[3].wait()
        for sample in range(samples):
            hop(sample).wait_send()
            for step in every:
                ahead(sample, step).wait_send()
            home(sample).wait_recv()
        for lend in lends:
            lend.wait_send()

    @pl.when(section == sections - 1)
    def _():
        for sample in range(samples):
            for step in steps:
                back(sample, step).wait_send()
            store(sample).wait()


def on_device(frames_in, spatial_qkv, spatial_out, temporal_qkv, temporal_out, modulation):
    samples, local_frames, patches, width = frames_in.shape
    assert local_frames == 1
    seq_count = lax.axis_size("seq")
    sections = lax.axis_size("section")
    head_width = spatial_out.shape[1]
    rows = patches // seq_count
    bf16, f32 = jnp.bfloat16, jnp.float32
    dma = pltpu.SemaphoreType.DMA
    anywhere = pl.BlockSpec(memory_space=pltpu.HBM)
    span = max(stop - start for start, stop, *_ in head_windows(head_width))
    hidden = pl.pallas_call(
        functools.partial(kernel, seq_count, sections),
        out_shape=jax.ShapeDtypeStruct((samples, patches, width), bf16),
        in_specs=[anywhere] * 6,
        out_specs=anywhere,
        scratch_shapes=[
            pltpu.VMEM(spatial_qkv.shape[:0:-1], bf16),
            pltpu.VMEM(spatial_out.shape[1:], bf16),
            pltpu.VMEM(temporal_qkv.shape[:0:-1], bf16),
            pltpu.VMEM(temporal_out.shape[1:], bf16),
            pltpu.VMEM((modulation.shape[2], samples, width), f32),
            pltpu.VMEM((samples, modulation.shape[2], width), f32),
            pltpu.VMEM(spatial_qkv.shape[1:], bf16),
            pltpu.VMEM(temporal_qkv.shape[1:], bf16),
            pltpu.VMEM(temporal_out.shape[1:], bf16),
            pltpu.VMEM((samples, width), f32),
            pltpu.VMEM((samples, 1, width), f32),
            pltpu.VMEM((samples, patches, width), bf16),
            pltpu.VMEM((samples, patches, width), bf16),
            pltpu.VMEM((samples, patches, width), bf16),
            pltpu.VMEM((patches, width), f32),
            pltpu.VMEM((samples, patches, width), f32),
            pltpu.VMEM((patches, 3 * head_width), f32),
            pltpu.VMEM((samples, seq_count, rows, width), bf16),
            pltpu.VMEM((samples, seq_count, rows, width), bf16),
            pltpu.VMEM((samples, seq_count, rows, head_width), bf16),
            pltpu.VMEM((samples, seq_count, rows, head_width), bf16),
            pltpu.VMEM((samples, seq_count, rows, head_width), bf16),
            pltpu.VMEM((HEADS // 2, 2 * patches, span), bf16),
            pltpu.VMEM((HEADS // 2, span, span), bf16),
            pltpu.VMEM((patches, 2 * patches), bf16),
            dma((4,)),
            dma((len(chunks(3 * head_width)),)),
            dma((samples,)),
            dma((samples,)),
            dma((2,)),
            dma((2,)),
            dma((samples,)),
            dma((samples,)),
            dma((samples, seq_count)),
            dma((samples, seq_count)),
            dma((samples, seq_count)),
            dma((samples, seq_count)),
            dma((samples, seq_count)),
            dma((samples, seq_count)),
            dma((samples,)),
            dma((samples,)),
        ],
        compiler_params=pltpu.CompilerParams(
            collective_id=0, has_side_effects=True, vmem_limit_bytes=60 * 1024 * 1024
        ),
    )(
        frames_in.reshape(samples, patches, width),
        jnp.swapaxes(spatial_qkv, 1, 2), spatial_out,
        jnp.swapaxes(temporal_qkv, 1, 2), temporal_out,
        jnp.swapaxes(modulation, 1, 2),
    )
    return hidden.reshape(1, samples, 1, patches, width)


def solution(mesh):
    placed = (
        P(None, "seq", None, None),
        P("section", None, None),
        P("section", None, None),
        P("section", None, None),
        P("section", None, None),
        P("section", None, None, None),
    )
    return jax.shard_map(
        on_device,
        mesh=mesh,
        in_specs=placed,
        out_specs=P("section", None, "seq", None, None),
        check_vma=False,
    )
```

```python
import functools
import math

import jax
import jax.numpy as jnp
from jax import lax
from jax.experimental import pallas as pl
from jax.experimental.pallas import tpu as pltpu
from jax.sharding import PartitionSpec as P

HEADS = 8
LANES = 128
CHUNK = 256
MESH = pl.DeviceIdType.MESH


def chunks(width, size=CHUNK):
    return [(at, min(at + size, width)) for at in range(0, width, size)]


def head_windows(head_width):
    size = head_width // HEADS
    found = []
    for pair in range(HEADS // 2):
        low, high = 2 * pair * size, 2 * (pair + 1) * size
        start = low // LANES * LANES
        stop = min(head_width, -(-high // LANES) * LANES)
        found.append((start, stop, low, low + size, high))
    return found


def gather_windows(head_width, parts):
    columns = []
    for low, high in chunks(head_width, LANES):
        total = None
        for (start, stop), part in parts:
            if start <= low and high <= stop:
                piece = part[:, low - start : high - start]
                total = piece if total is None else total + piece
        columns.append(total)
    return jnp.concatenate(columns, axis=1)


def flipped(index, step, count):
    total, bit = 0, 1
    while bit < count:
        total = total + lax.rem(index // bit + step // bit, 2) * bit
        bit *= 2
    return total


def norm_modulate(residual, offset, scaling):
    near = residual - jnp.mean(residual[:, :CHUNK], axis=-1, keepdims=True)
    rest = jnp.mean(near, axis=-1, keepdims=True)
    variance = jnp.mean(near * near, axis=-1, keepdims=True) - rest * rest
    return (near - rest) * lax.rsqrt(variance + 1e-06) * (1.0 + scaling) + offset


def split_rows(tensor, count):
    rows = tensor.shape[0] // count
    return [tensor[r * rows : (r + 1) * rows].astype(jnp.bfloat16) for r in range(count)]


def join_rows(ref, sample):
    _, count, rows, width = ref.shape
    if rows % 16 == 0:
        return ref[sample].reshape(count * rows, width)
    parts = [ref[sample, r].astype(jnp.float32) for r in range(count)]
    return jnp.concatenate(parts, axis=0).astype(jnp.bfloat16)


def kernel(
    seq_count, sections,
    frames_hbm, sqkv_hbm, sout_hbm, tqkv_hbm, tout_hbm, mod_hbm,
    hidden_hbm,
    sqkv, sout, tqkv, tout, mod, factors, sqkv_across, tqkv_across, tout_before, gate_before, gates,
    x_in, x_out, y_out, residual, middle, qkv, sent, arrived, mixed_sent, returned, handed,
    pair_mask, square_mask, patch_mask,
    load_sem, first_sem, frame_sem, store_sem, lend_send, lend_recv,
    hop_send, hop_recv, go_send, go_recv, back_send, back_recv, ahead_send, ahead_recv,
    home_send, home_recv,
):
    samples, patches, width = x_in.shape
    head_width = sout.shape[0]
    head_size = head_width // HEADS
    windows = head_windows(head_width)
    section = lax.axis_index("section")
    me = lax.axis_index("seq")
    peers = [flipped(me, step, seq_count) for step in range(seq_count)]
    after = lax.rem(section + 1, sections)
    before = lax.rem(section + sections - 1, sections)

    loads = [
        pltpu.make_async_copy(src.at[0], dst, load_sem.at[at])
        for at, (src, dst) in enumerate(
            ((mod_hbm, mod), (sout_hbm, sout), (tqkv_hbm, tqkv), (tout_hbm, tout))
        )
    ]

    def frame_load(sample):
        return pltpu.make_async_copy(
            frames_hbm.at[sample], x_in.at[sample], frame_sem.at[sample]
        )

    @pl.when(section == 0)
    def _():
        frame_load(0).start()

    first_loads = [
        pltpu.make_async_copy(
            sqkv_hbm.at[0, pl.ds(low, high - low)], sqkv.at[pl.ds(low, high - low)], first_sem.at[at]
        )
        for at, (low, high) in enumerate(chunks(3 * head_width))
    ]
    loads[0].start()
    for load in first_loads:
        load.start()
    loads[1].start()

    barrier = pltpu.get_barrier_semaphore()
    for step in range(1, seq_count):
        pl.semaphore_signal(
            barrier, inc=1, device_id={"seq": peers[step]}, device_id_type=MESH
        )
    def greet(step):
        for other in range(seq_count):
            pl.semaphore_signal(
                barrier, inc=1,
                device_id={"section": section + step, "seq": other}, device_id_type=MESH,
            )

    @pl.when(section > 0)
    def _():
        greet(-1)

    @pl.when(section < sections - 1)
    def _():
        greet(1)

    for at, (start, stop, low, center, high) in enumerate(windows):
        span = stop - start
        lane = lax.broadcasted_iota(jnp.int32, (2 * patches, span), 1) + start
        row = lax.broadcasted_iota(jnp.int32, (2 * patches, span), 0)
        first = jnp.where((lane >= low) & (lane < center), 1.0, 0.0)
        second = jnp.where((lane >= center) & (lane < high), 1.0, 0.0)
        pair_mask[at, :, :span] = jnp.where(row < patches, first, second).astype(jnp.bfloat16)
        lane = lax.broadcasted_iota(jnp.int32, (span, span), 1) + start
        row = lax.broadcasted_iota(jnp.int32, (span, span), 0) + start
        first = (lane >= low) & (lane < center) & (row >= low) & (row < center)
        second = (lane >= center) & (lane < high) & (row >= center) & (row < high)
        square_mask[at, :span, :span] = jnp.where(
            first, 1.0, jnp.where(second, 1.0, 0.0)
        ).astype(jnp.bfloat16)
    group = patches // seq_count
    row = lax.broadcasted_iota(jnp.int32, (patches, 2 * patches), 0)
    lane = lax.broadcasted_iota(jnp.int32, (patches, 2 * patches), 1)
    patch_mask[...] = jnp.where(
        lax.rem(row, group) == lax.rem(lane, group), 1.0, 0.0
    ).astype(jnp.bfloat16)

    def turn(load, stored, across):
        load.wait()
        for low, high in chunks(3 * head_width):
            across[:, low:high] = stored[low:high, :].T

    @pl.when(section == 0)
    def _():
        tout_before[...] = jnp.zeros_like(tout_before)
        handed[...] = jnp.zeros_like(handed)
        gates[...] = jnp.zeros_like(gates)

    for load, (low, high) in zip(first_loads, chunks(3 * head_width)):
        load.wait()
        sqkv_across[:, low:high] = sqkv[low:high, :].T
    for load in loads[2:]:
        load.start()

    @pl.when(section == 0)
    def _():
        for sample in range(1, samples):
            frame_load(sample).start()

    beside = jnp.minimum(section, 1) + jnp.minimum(sections - 1 - section, 1)
    pl.semaphore_wait(barrier, seq_count - 1 + seq_count * beside)

    def following(seq=None):
        place = {"section": after}
        if seq is not None:
            place["seq"] = seq
        return place

    lends = [
        pltpu.make_async_remote_copy(
            src_ref=src, dst_ref=dst, send_sem=lend_send.at[at], recv_sem=lend_recv.at[at],
            device_id=following(), device_id_type=MESH,
        )
        for at, (src, dst) in enumerate(
            ((tout_hbm.at[0], tout_before), (mod_hbm.at[0, mod.shape[0] - 1], gate_before))
        )
    ]

    @pl.when(section < sections - 1)
    def _():
        for lend in lends:
            lend.start()

    @pl.when(section > 0)
    def _():
        turn(loads[2], tqkv, tqkv_across)

    def factor(sample, row, low=0, high=width):
        return factors[sample, row : row + 1, low:high]

    def project(rows, across):
        blocks = chunks(3 * head_width)
        keys = [b for b in blocks if b[1] > head_width and b[0] < 2 * head_width]
        for low, high in keys + [b for b in blocks if b not in keys]:
            qkv[:, low:high] = jnp.dot(
                rows, across[:, low:high], preferred_element_type=jnp.float32
            )

    def head_norms(tensor):
        squares = (tensor * tensor).astype(jnp.bfloat16)
        parts = []
        for at, (start, stop, *_) in enumerate(windows):
            span = stop - start
            parts.append(((start, stop), jnp.dot(
                squares[:, start:stop], square_mask[at, :span, :span],
                preferred_element_type=jnp.float32,
            )))
        return lax.rsqrt(gather_windows(head_width, parts) * (1.0 / head_size) + 1e-06)

    def attend(same_patch):
        queries = qkv[:, :head_width]
        aligned = head_width // LANES * LANES
        lookups = qkv[:, aligned : 2 * head_width]
        if aligned != head_width:
            reach = 2 * head_width - aligned
            lookups = pltpu.roll(lookups, reach - (head_width - aligned), 1)[:, :head_width]
        values = qkv[:, 2 * head_width :].astype(jnp.bfloat16)
        lookups = (lookups * head_norms(lookups)).astype(jnp.bfloat16)
        scale = math.log2(math.e) / math.sqrt(head_size)
        queries = (queries * (head_norms(queries) * scale)).astype(jnp.bfloat16)
        exponents = []
        for at, (start, stop, *_) in enumerate(windows):
            part = lookups[:, start:stop]
            both = jnp.concatenate([part, part], axis=0) * pair_mask[at, :, : stop - start]
            exponents.append(lax.dot_general(
                queries[:, start:stop], both, (((1,), (1,)), ((), ())),
                preferred_element_type=jnp.float32,
            ))
        exponents = [jnp.exp2(scores).astype(jnp.bfloat16) for scores in exponents]
        if same_patch:
            exponents = [exponent * patch_mask[...] for exponent in exponents]
        tops, bottoms = [], []
        for at, (start, stop, *_) in enumerate(windows):
            mask = pair_mask[at, :, : stop - start]
            part = values[:, start:stop]
            both = jnp.concatenate([part, part], axis=0) * mask
            bottoms.append(((start, stop), jnp.dot(
                exponents[at], mask, preferred_element_type=jnp.float32
            )))
            tops.append(((start, stop), jnp.dot(
                exponents[at], both, preferred_element_type=jnp.float32
            )))
        return gather_windows(head_width, tops) / gather_windows(head_width, bottoms)

    def exchange(source, target, send_sem, recv_sem, sample, step):
        peer = peers[step]
        return pltpu.make_async_remote_copy(
            src_ref=source.at[sample, peer],
            dst_ref=target.at[sample, me],
            send_sem=send_sem.at[sample, step],
            recv_sem=recv_sem.at[sample, step],
            device_id={"seq": peer},
            device_id_type=MESH,
        )

    def go(sample, step):
        return exchange(sent, arrived, go_send, go_recv, sample, step)

    def back(sample, step):
        return exchange(mixed_sent, returned, back_send, back_recv, sample, step)

    def hop(sample):
        return pltpu.make_async_remote_copy(
            src_ref=y_out.at[sample],
            dst_ref=x_in.at[sample],
            send_sem=hop_send.at[sample],
            recv_sem=hop_recv.at[sample],
            device_id=following(),
            device_id_type=MESH,
        )

    def ahead(sample, step):
        peer = peers[step]
        return pltpu.make_async_remote_copy(
            src_ref=mixed_sent.at[sample, peer],
            dst_ref=handed.at[sample, me],
            send_sem=ahead_send.at[sample, step],
            recv_sem=ahead_recv.at[sample, step],
            device_id=following(peer),
            device_id_type=MESH,
        )

    def home(sample):
        return pltpu.make_async_remote_copy(
            src_ref=x_out.at[sample],
            dst_ref=hidden_hbm.at[sample],
            send_sem=home_send.at[sample],
            recv_sem=home_recv.at[sample],
            device_id={"section": before},
            device_id_type=MESH,
        )

    def store(sample):
        return pltpu.make_async_copy(
            y_out.at[sample], hidden_hbm.at[sample], store_sem.at[sample]
        )

    steps = range(seq_count - 1, 0, -1)
    every = range(seq_count - 1, -1, -1)

    def spatial(sample):
        @pl.when(sample == 0)
        def _():
            loads[0].wait()
            loads[1].wait()
            for video in range(samples):
                for row in range(mod.shape[0]):
                    factors[video, row : row + 1, :] = mod[row, video : video + 1, :]

        @pl.when(section == 0)
        def _():
            frame_load(sample).wait()

        @pl.when(section > 0)
        def _():
            @pl.when(sample == 0)
            def _():
                for lend in lends:
                    lend.wait_recv()
                for video in range(samples):
                    gates[video] = gate_before[video : video + 1, :]

            hop(sample).wait_recv()
            for step in every:
                ahead(sample, step).wait_recv()

        mixed = join_rows(handed, sample)
        for low, high in chunks(width):
            residual[:, low:high] = x_in[sample, :, low:high].astype(jnp.float32) + gates[
                sample, :, low:high
            ] * jnp.dot(mixed, tout_before[:, low:high], preferred_element_type=jnp.float32)

        normed = norm_modulate(residual[...], factor(sample, 0), factor(sample, 1))
        project(normed.astype(jnp.bfloat16), sqkv_across)
        mixed = attend(False).astype(jnp.bfloat16)

        for low, high in chunks(width):
            middle[sample, :, low:high] = residual[:, low:high] + factor(
                sample, 2, low, high
            ) * jnp.dot(mixed, sout[:, low:high], preferred_element_type=jnp.float32)
        payload = norm_modulate(middle[sample], factor(sample, 3), factor(sample, 4))
        for at, part in enumerate(split_rows(payload, seq_count)):
            sent[sample, at] = part
        for step in steps:
            go(sample, step).start()
        arrived[sample, me] = sent[sample, me]
        y_out[sample] = middle[sample].astype(jnp.bfloat16)

        x_out[sample] = residual[...].astype(jnp.bfloat16)

    def temporal(sample):
        for step in steps:
            go(sample, step).wait_recv()
        project(join_rows(arrived, sample), tqkv_across)
        for at, part in enumerate(split_rows(attend(True), seq_count)):
            mixed_sent[sample, at] = part

        @pl.when(section < sections - 1)
        def _():
            for step in every:
                ahead(sample, step).start()

        @pl.when(section == sections - 1)
        def _():
            for step in steps:
                back(sample, step).start()
            returned[sample, me] = mixed_sent[sample, me]

    def finish(sample):
        @pl.when(sample == 0)
        def _():
            loads[3].wait()

        for step in steps:
            back(sample, step).wait_recv()
        mixed = join_rows(returned, sample)
        for low, high in chunks(width):
            y_out[sample, :, low:high] = (
                middle[sample, :, low:high]
                + factor(sample, 5, low, high)
                * jnp.dot(mixed, tout[:, low:high], preferred_element_type=jnp.float32)
            ).astype(jnp.bfloat16)

        store(sample).start()

    @pl.loop(0, samples + 1)
    def _(at):
        @pl.when(at < samples)
        def _():
            spatial(at)

        @pl.when((at == 0) & (section == 0))
        def _():
            turn(loads[2], tqkv, tqkv_across)

        @pl.when(at > 0)
        def _():
            temporal(at - 1)

        @pl.when((at < samples) & (section < sections - 1))
        def _():
            hop(at).start()

        @pl.when((at < samples) & (section > 0))
        def _():
            home(at).start()

    @pl.when(section == sections - 1)
    def _():
        @pl.loop(0, samples)
        def _(at):
            finish(at)

    for sample in range(samples):
        for step in steps:
            go(sample, step).wait_send()

    @pl.when(section > 0)
    def _():
        for sample in range(samples):
            home(sample).wait_send()

    @pl.when(section < sections - 1)
    def _():
        loads[3].wait()
        for sample in range(samples):
            hop(sample).wait_send()
            for step in every:
                ahead(sample, step).wait_send()
            home(sample).wait_recv()
        for lend in lends:
            lend.wait_send()

    @pl.when(section == sections - 1)
    def _():
        for sample in range(samples):
            for step in steps:
                back(sample, step).wait_send()
            store(sample).wait()


def on_device(frames_in, spatial_qkv, spatial_out, temporal_qkv, temporal_out, modulation):
    samples, local_frames, patches, width = frames_in.shape
    assert local_frames == 1
    seq_count = lax.axis_size("seq")
    sections = lax.axis_size("section")
    head_width = spatial_out.shape[1]
    rows = patches // seq_count
    bf16, f32 = jnp.bfloat16, jnp.float32
    dma = pltpu.SemaphoreType.DMA
    anywhere = pl.BlockSpec(memory_space=pltpu.HBM)
    span = max(stop - start for start, stop, *_ in head_windows(head_width))
    hidden = pl.pallas_call(
        functools.partial(kernel, seq_count, sections),
        out_shape=jax.ShapeDtypeStruct((samples, patches, width), bf16),
        in_specs=[anywhere] * 6,
        out_specs=anywhere,
        scratch_shapes=[
            pltpu.VMEM(spatial_qkv.shape[:0:-1], bf16),
            pltpu.VMEM(spatial_out.shape[1:], bf16),
            pltpu.VMEM(temporal_qkv.shape[:0:-1], bf16),
            pltpu.VMEM(temporal_out.shape[1:], bf16),
            pltpu.VMEM((modulation.shape[2], samples, width), f32),
            pltpu.VMEM((samples, modulation.shape[2], width), f32),
            pltpu.VMEM(spatial_qkv.shape[1:], bf16),
            pltpu.VMEM(temporal_qkv.shape[1:], bf16),
            pltpu.VMEM(temporal_out.shape[1:], bf16),
            pltpu.VMEM((samples, width), f32),
            pltpu.VMEM((samples, 1, width), f32),
            pltpu.VMEM((samples, patches, width), bf16),
            pltpu.VMEM((samples, patches, width), bf16),
            pltpu.VMEM((samples, patches, width), bf16),
            pltpu.VMEM((patches, width), f32),
            pltpu.VMEM((samples, patches, width), f32),
            pltpu.VMEM((patches, 3 * head_width), f32),
            pltpu.VMEM((samples, seq_count, rows, width), bf16),
            pltpu.VMEM((samples, seq_count, rows, width), bf16),
            pltpu.VMEM((samples, seq_count, rows, head_width), bf16),
            pltpu.VMEM((samples, seq_count, rows, head_width), bf16),
            pltpu.VMEM((samples, seq_count, rows, head_width), bf16),
            pltpu.VMEM((HEADS // 2, 2 * patches, span), bf16),
            pltpu.VMEM((HEADS // 2, span, span), bf16),
            pltpu.VMEM((patches, 2 * patches), bf16),
            dma((4,)),
            dma((len(chunks(3 * head_width)),)),
            dma((samples,)),
            dma((samples,)),
            dma((2,)),
            dma((2,)),
            dma((samples,)),
            dma((samples,)),
            dma((samples, seq_count)),
            dma((samples, seq_count)),
            dma((samples, seq_count)),
            dma((samples, seq_count)),
            dma((samples, seq_count)),
            dma((samples, seq_count)),
            dma((samples,)),
            dma((samples,)),
        ],
        compiler_params=pltpu.CompilerParams(
            collective_id=0, has_side_effects=True, vmem_limit_bytes=60 * 1024 * 1024
        ),
    )(
        frames_in.reshape(samples, patches, width),
        jnp.swapaxes(spatial_qkv, 1, 2), spatial_out,
        jnp.swapaxes(temporal_qkv, 1, 2), temporal_out,
        jnp.swapaxes(modulation, 1, 2),
    )
    return hidden.reshape(1, samples, 1, patches, width)


def solution(mesh):
    placed = (
        P(None, "seq", None, None),
        P("section", None, None),
        P("section", None, None),
        P("section", None, None),
        P("section", None, None),
        P("section", None, None, None),
    )
    return jax.shard_map(
        on_device,
        mesh=mesh,
        in_specs=placed,
        out_specs=P("section", None, "seq", None, None),
        check_vma=False,
    )
```

```python
import functools
import math

import jax
import jax.numpy as jnp
from jax import lax
from jax.experimental import pallas as pl
from jax.experimental.pallas import tpu as pltpu
from jax.sharding import PartitionSpec as P

HEADS = 8
LANES = 128
CHUNK = 256
MESH = pl.DeviceIdType.MESH


def chunks(width, size=CHUNK):
    return [(at, min(at + size, width)) for at in range(0, width, size)]


def head_windows(head_width):
    size = head_width // HEADS
    found = []
    for pair in range(HEADS // 2):
        low, high = 2 * pair * size, 2 * (pair + 1) * size
        start = low // LANES * LANES
        stop = min(head_width, -(-high // LANES) * LANES)
        found.append((start, stop, low, low + size, high))
    return found


def gather_windows(head_width, parts):
    columns = []
    for low, high in chunks(head_width, LANES):
        total = None
        for (start, stop), part in parts:
            if start <= low and high <= stop:
                piece = part[:, low - start : high - start]
                total = piece if total is None else total + piece
        columns.append(total)
    return jnp.concatenate(columns, axis=1)


def flipped(index, step, count):
    total, bit = 0, 1
    while bit < count:
        total = total + lax.rem(index // bit + step // bit, 2) * bit
        bit *= 2
    return total


def norm_modulate(residual, offset, scaling):
    near = residual - jnp.mean(residual[:, :CHUNK], axis=-1, keepdims=True)
    rest = jnp.mean(near, axis=-1, keepdims=True)
    variance = jnp.mean(near * near, axis=-1, keepdims=True) - rest * rest
    return (near - rest) * lax.rsqrt(variance + 1e-06) * (1.0 + scaling) + offset


def split_rows(tensor, count):
    rows = tensor.shape[0] // count
    return [tensor[r * rows : (r + 1) * rows].astype(jnp.bfloat16) for r in range(count)]


def join_rows(ref, sample):
    _, count, rows, width = ref.shape
    if rows % 16 == 0:
        return ref[sample].reshape(count * rows, width)
    parts = [ref[sample, r].astype(jnp.float32) for r in range(count)]
    return jnp.concatenate(parts, axis=0).astype(jnp.bfloat16)


def kernel(
    seq_count, sections,
    frames_hbm, sqkv_hbm, sout_hbm, tqkv_hbm, tout_hbm, mod_hbm,
    hidden_hbm,
    sqkv, sout, tqkv, tout, mod, factors, sqkv_across, tqkv_across, tout_before, gate_before, gates,
    x_in, x_out, y_out, residual, middle, qkv, sent, arrived, mixed_sent, returned, handed,
    pair_mask, square_mask, patch_mask,
    load_sem, first_sem, frame_sem, store_sem, lend_send, lend_recv,
    hop_send, hop_recv, go_send, go_recv, back_send, back_recv, ahead_send, ahead_recv,
    home_send, home_recv,
):
    samples, patches, width = x_in.shape
    head_width = sout.shape[0]
    head_size = head_width // HEADS
    windows = head_windows(head_width)
    section = lax.axis_index("section")
    me = lax.axis_index("seq")
    peers = [flipped(me, step, seq_count) for step in range(seq_count)]
    after = lax.rem(section + 1, sections)
    before = lax.rem(section + sections - 1, sections)

    loads = [
        pltpu.make_async_copy(src.at[0], dst, load_sem.at[at])
        for at, (src, dst) in enumerate(
            ((mod_hbm, mod), (sout_hbm, sout), (tqkv_hbm, tqkv), (tout_hbm, tout))
        )
    ]

    def frame_load(sample):
        return pltpu.make_async_copy(
            frames_hbm.at[sample], x_in.at[sample], frame_sem.at[sample]
        )

    @pl.when(section == 0)
    def _():
        frame_load(0).start()

    first_loads = [
        pltpu.make_async_copy(
            sqkv_hbm.at[0, pl.ds(low, high - low)], sqkv.at[pl.ds(low, high - low)], first_sem.at[at]
        )
        for at, (low, high) in enumerate(chunks(3 * head_width))
    ]
    loads[0].start()
    for load in first_loads:
        load.start()
    loads[1].start()

    barrier = pltpu.get_barrier_semaphore()
    for step in range(1, seq_count):
        pl.semaphore_signal(
            barrier, inc=1, device_id={"seq": peers[step]}, device_id_type=MESH
        )
    def greet(step):
        for other in range(seq_count):
            pl.semaphore_signal(
                barrier, inc=1,
                device_id={"section": section + step, "seq": other}, device_id_type=MESH,
            )

    @pl.when(section > 0)
    def _():
        greet(-1)

    @pl.when(section < sections - 1)
    def _():
        greet(1)

    for at, (start, stop, low, center, high) in enumerate(windows):
        span = stop - start
        lane = lax.broadcasted_iota(jnp.int32, (2 * patches, span), 1) + start
        row = lax.broadcasted_iota(jnp.int32, (2 * patches, span), 0)
        first = jnp.where((lane >= low) & (lane < center), 1.0, 0.0)
        second = jnp.where((lane >= center) & (lane < high), 1.0, 0.0)
        pair_mask[at, :, :span] = jnp.where(row < patches, first, second).astype(jnp.bfloat16)
        lane = lax.broadcasted_iota(jnp.int32, (span, span), 1) + start
        row = lax.broadcasted_iota(jnp.int32, (span, span), 0) + start
        first = (lane >= low) & (lane < center) & (row >= low) & (row < center)
        second = (lane >= center) & (lane < high) & (row >= center) & (row < high)
        square_mask[at, :span, :span] = jnp.where(
            first, 1.0, jnp.where(second, 1.0, 0.0)
        ).astype(jnp.bfloat16)
    group = patches // seq_count
    row = lax.broadcasted_iota(jnp.int32, (patches, 2 * patches), 0)
    lane = lax.broadcasted_iota(jnp.int32, (patches, 2 * patches), 1)
    patch_mask[...] = jnp.where(
        lax.rem(row, group) == lax.rem(lane, group), 1.0, 0.0
    ).astype(jnp.bfloat16)

    def turn(load, stored, across):
        load.wait()
        for low, high in chunks(3 * head_width):
            across[:, low:high] = stored[low:high, :].T

    @pl.when(section == 0)
    def _():
        tout_before[...] = jnp.zeros_like(tout_before)
        handed[...] = jnp.zeros_like(handed)
        gates[...] = jnp.zeros_like(gates)

    for load, (low, high) in zip(first_loads, chunks(3 * head_width)):
        load.wait()
        sqkv_across[:, low:high] = sqkv[low:high, :].T
    for load in loads[2:]:
        load.start()

    @pl.when(section == 0)
    def _():
        for sample in range(1, samples):
            frame_load(sample).start()

    beside = jnp.minimum(section, 1) + jnp.minimum(sections - 1 - section, 1)
    pl.semaphore_wait(barrier, seq_count - 1 + seq_count * beside)

    def following(seq=None):
        place = {"section": after}
        if seq is not None:
            place["seq"] = seq
        return place

    lends = [
        pltpu.make_async_remote_copy(
            src_ref=src, dst_ref=dst, send_sem=lend_send.at[at], recv_sem=lend_recv.at[at],
            device_id=following(), device_id_type=MESH,
        )
        for at, (src, dst) in enumerate(
            ((tout_hbm.at[0], tout_before), (mod_hbm.at[0, mod.shape[0] - 1], gate_before))
        )
    ]

    @pl.when(section < sections - 1)
    def _():
        for lend in lends:
            lend.start()

    @pl.when(section > 0)
    def _():
        turn(loads[2], tqkv, tqkv_across)

    def factor(sample, row, low=0, high=width):
        return factors[sample, row : row + 1, low:high]

    def project(rows, across):
        blocks = chunks(3 * head_width)
        keys = [b for b in blocks if b[1] > head_width and b[0] < 2 * head_width]
        for low, high in keys + [b for b in blocks if b not in keys]:
            qkv[:, low:high] = jnp.dot(
                rows, across[:, low:high], preferred_element_type=jnp.float32
            )

    def head_norms(tensor):
        squares = (tensor * tensor).astype(jnp.bfloat16)
        parts = []
        for at, (start, stop, *_) in enumerate(windows):
            span = stop - start
            parts.append(((start, stop), jnp.dot(
                squares[:, start:stop], square_mask[at, :span, :span],
                preferred_element_type=jnp.float32,
            )))
        return lax.rsqrt(gather_windows(head_width, parts) * (1.0 / head_size) + 1e-06)

    def attend(same_patch):
        queries = qkv[:, :head_width]
        aligned = head_width // LANES * LANES
        lookups = qkv[:, aligned : 2 * head_width]
        if aligned != head_width:
            reach = 2 * head_width - aligned
            lookups = pltpu.roll(lookups, reach - (head_width - aligned), 1)[:, :head_width]
        values = qkv[:, 2 * head_width :].astype(jnp.bfloat16)
        lookups = (lookups * head_norms(lookups)).astype(jnp.bfloat16)
        scale = math.log2(math.e) / math.sqrt(head_size)
        queries = (queries * (head_norms(queries) * scale)).astype(jnp.bfloat16)
        exponents = []
        for at, (start, stop, *_) in enumerate(windows):
            part = lookups[:, start:stop]
            both = jnp.concatenate([part, part], axis=0) * pair_mask[at, :, : stop - start]
            exponents.append(lax.dot_general(
                queries[:, start:stop], both, (((1,), (1,)), ((), ())),
                preferred_element_type=jnp.float32,
            ))
        exponents = [jnp.exp2(scores).astype(jnp.bfloat16) for scores in exponents]
        if same_patch:
            exponents = [exponent * patch_mask[...] for exponent in exponents]
        tops, bottoms = [], []
        for at, (start, stop, *_) in enumerate(windows):
            mask = pair_mask[at, :, : stop - start]
            part = values[:, start:stop]
            both = jnp.concatenate([part, part], axis=0) * mask
            bottoms.append(((start, stop), jnp.dot(
                exponents[at], mask, preferred_element_type=jnp.float32
            )))
            tops.append(((start, stop), jnp.dot(
                exponents[at], both, preferred_element_type=jnp.float32
            )))
        return gather_windows(head_width, tops) / gather_windows(head_width, bottoms)

    def exchange(source, target, send_sem, recv_sem, sample, step):
        peer = peers[step]
        return pltpu.make_async_remote_copy(
            src_ref=source.at[sample, peer],
            dst_ref=target.at[sample, me],
            send_sem=send_sem.at[sample, step],
            recv_sem=recv_sem.at[sample, step],
            device_id={"seq": peer},
            device_id_type=MESH,
        )

    def go(sample, step):
        return exchange(sent, arrived, go_send, go_recv, sample, step)

    def back(sample, step):
        return exchange(mixed_sent, returned, back_send, back_recv, sample, step)

    def hop(sample):
        return pltpu.make_async_remote_copy(
            src_ref=y_out.at[sample],
            dst_ref=x_in.at[sample],
            send_sem=hop_send.at[sample],
            recv_sem=hop_recv.at[sample],
            device_id=following(),
            device_id_type=MESH,
        )

    def ahead(sample, step):
        peer = peers[step]
        return pltpu.make_async_remote_copy(
            src_ref=mixed_sent.at[sample, peer],
            dst_ref=handed.at[sample, me],
            send_sem=ahead_send.at[sample, step],
            recv_sem=ahead_recv.at[sample, step],
            device_id=following(peer),
            device_id_type=MESH,
        )

    def home(sample):
        return pltpu.make_async_remote_copy(
            src_ref=x_out.at[sample],
            dst_ref=hidden_hbm.at[sample],
            send_sem=home_send.at[sample],
            recv_sem=home_recv.at[sample],
            device_id={"section": before},
            device_id_type=MESH,
        )

    def store(sample, low, high):
        columns = pl.ds(low, high - low)
        return pltpu.make_async_copy(
            y_out.at[sample, :, columns], hidden_hbm.at[sample, :, columns],
            store_sem.at[sample, low // CHUNK],
        )

    steps = range(seq_count - 1, 0, -1)
    every = range(seq_count - 1, -1, -1)

    def spatial(sample):
        @pl.when(sample == 0)
        def _():
            loads[0].wait()
            loads[1].wait()
            for video in range(samples):
                for row in range(mod.shape[0]):
                    factors[video, row : row + 1, :] = mod[row, video : video + 1, :]

        @pl.when(section == 0)
        def _():
            frame_load(sample).wait()

        @pl.when(section > 0)
        def _():
            @pl.when(sample == 0)
            def _():
                for lend in lends:
                    lend.wait_recv()
                for video in range(samples):
                    gates[video] = gate_before[video : video + 1, :]

            hop(sample).wait_recv()
            for step in every:
                ahead(sample, step).wait_recv()

        mixed = join_rows(handed, sample)
        for low, high in chunks(width):
            residual[:, low:high] = x_in[sample, :, low:high].astype(jnp.float32) + gates[
                sample, :, low:high
            ] * jnp.dot(mixed, tout_before[:, low:high], preferred_element_type=jnp.float32)

        normed = norm_modulate(residual[...], factor(sample, 0), factor(sample, 1))
        project(normed.astype(jnp.bfloat16), sqkv_across)
        mixed = attend(False).astype(jnp.bfloat16)

        for low, high in chunks(width):
            middle[sample, :, low:high] = residual[:, low:high] + factor(
                sample, 2, low, high
            ) * jnp.dot(mixed, sout[:, low:high], preferred_element_type=jnp.float32)
        payload = norm_modulate(middle[sample], factor(sample, 3), factor(sample, 4))
        for at, part in enumerate(split_rows(payload, seq_count)):
            sent[sample, at] = part
        for step in steps:
            go(sample, step).start()
        arrived[sample, me] = sent[sample, me]
        y_out[sample] = middle[sample].astype(jnp.bfloat16)

        x_out[sample] = residual[...].astype(jnp.bfloat16)

    def temporal(sample):
        for step in steps:
            go(sample, step).wait_recv()
        project(join_rows(arrived, sample), tqkv_across)
        for at, part in enumerate(split_rows(attend(True), seq_count)):
            mixed_sent[sample, at] = part

        @pl.when(section < sections - 1)
        def _():
            for step in every:
                ahead(sample, step).start()

        @pl.when(section == sections - 1)
        def _():
            for step in steps:
                back(sample, step).start()
            returned[sample, me] = mixed_sent[sample, me]

    def finish(sample):
        @pl.when(sample == 0)
        def _():
            loads[3].wait()

        for step in steps:
            back(sample, step).wait_recv()
        mixed = join_rows(returned, sample)
        for low, high in chunks(width):
            y_out[sample, :, low:high] = (
                middle[sample, :, low:high]
                + factor(sample, 5, low, high)
                * jnp.dot(mixed, tout[:, low:high], preferred_element_type=jnp.float32)
            ).astype(jnp.bfloat16)
            store(sample, low, high).start()

    @pl.loop(0, samples + 1)
    def _(at):
        @pl.when(at < samples)
        def _():
            spatial(at)

        @pl.when((at == 0) & (section == 0))
        def _():
            turn(loads[2], tqkv, tqkv_across)

        @pl.when(at > 0)
        def _():
            temporal(at - 1)

        @pl.when((at < samples) & (section < sections - 1))
        def _():
            hop(at).start()

        @pl.when((at < samples) & (section > 0))
        def _():
            home(at).start()

    @pl.when(section == sections - 1)
    def _():
        @pl.loop(0, samples)
        def _(at):
            finish(at)

    for sample in range(samples):
        for step in steps:
            go(sample, step).wait_send()

    @pl.when(section > 0)
    def _():
        for sample in range(samples):
            home(sample).wait_send()

    @pl.when(section < sections - 1)
    def _():
        loads[3].wait()
        for sample in range(samples):
            hop(sample).wait_send()
            for step in every:
                ahead(sample, step).wait_send()
            home(sample).wait_recv()
        for lend in lends:
            lend.wait_send()

    @pl.when(section == sections - 1)
    def _():
        for sample in range(samples):
            for step in steps:
                back(sample, step).wait_send()
            for low, high in chunks(width):
                store(sample, low, high).wait()


def on_device(frames_in, spatial_qkv, spatial_out, temporal_qkv, temporal_out, modulation):
    samples, local_frames, patches, width = frames_in.shape
    assert local_frames == 1
    seq_count = lax.axis_size("seq")
    sections = lax.axis_size("section")
    head_width = spatial_out.shape[1]
    rows = patches // seq_count
    bf16, f32 = jnp.bfloat16, jnp.float32
    dma = pltpu.SemaphoreType.DMA
    anywhere = pl.BlockSpec(memory_space=pltpu.HBM)
    span = max(stop - start for start, stop, *_ in head_windows(head_width))
    hidden = pl.pallas_call(
        functools.partial(kernel, seq_count, sections),
        out_shape=jax.ShapeDtypeStruct((samples, patches, width), bf16),
        in_specs=[anywhere] * 6,
        out_specs=anywhere,
        scratch_shapes=[
            pltpu.VMEM(spatial_qkv.shape[:0:-1], bf16),
            pltpu.VMEM(spatial_out.shape[1:], bf16),
            pltpu.VMEM(temporal_qkv.shape[:0:-1], bf16),
            pltpu.VMEM(temporal_out.shape[1:], bf16),
            pltpu.VMEM((modulation.shape[2], samples, width), f32),
            pltpu.VMEM((samples, modulation.shape[2], width), f32),
            pltpu.VMEM(spatial_qkv.shape[1:], bf16),
            pltpu.VMEM(temporal_qkv.shape[1:], bf16),
            pltpu.VMEM(temporal_out.shape[1:], bf16),
            pltpu.VMEM((samples, width), f32),
            pltpu.VMEM((samples, 1, width), f32),
            pltpu.VMEM((samples, patches, width), bf16),
            pltpu.VMEM((samples, patches, width), bf16),
            pltpu.VMEM((samples, patches, width), bf16),
            pltpu.VMEM((patches, width), f32),
            pltpu.VMEM((samples, patches, width), f32),
            pltpu.VMEM((patches, 3 * head_width), f32),
            pltpu.VMEM((samples, seq_count, rows, width), bf16),
            pltpu.VMEM((samples, seq_count, rows, width), bf16),
            pltpu.VMEM((samples, seq_count, rows, head_width), bf16),
            pltpu.VMEM((samples, seq_count, rows, head_width), bf16),
            pltpu.VMEM((samples, seq_count, rows, head_width), bf16),
            pltpu.VMEM((HEADS // 2, 2 * patches, span), bf16),
            pltpu.VMEM((HEADS // 2, span, span), bf16),
            pltpu.VMEM((patches, 2 * patches), bf16),
            dma((4,)),
            dma((len(chunks(3 * head_width)),)),
            dma((samples,)),
            dma((samples, len(chunks(width)))),
            dma((2,)),
            dma((2,)),
            dma((samples,)),
            dma((samples,)),
            dma((samples, seq_count)),
            dma((samples, seq_count)),
            dma((samples, seq_count)),
            dma((samples, seq_count)),
            dma((samples, seq_count)),
            dma((samples, seq_count)),
            dma((samples,)),
            dma((samples,)),
        ],
        compiler_params=pltpu.CompilerParams(
            collective_id=0, has_side_effects=True, vmem_limit_bytes=60 * 1024 * 1024
        ),
    )(
        frames_in.reshape(samples, patches, width),
        jnp.swapaxes(spatial_qkv, 1, 2), spatial_out,
        jnp.swapaxes(temporal_qkv, 1, 2), temporal_out,
        jnp.swapaxes(modulation, 1, 2),
    )
    return hidden.reshape(1, samples, 1, patches, width)


def solution(mesh):
    placed = (
        P(None, "seq", None, None),
        P("section", None, None),
        P("section", None, None),
        P("section", None, None),
        P("section", None, None),
        P("section", None, None, None),
    )
    return jax.shard_map(
        on_device,
        mesh=mesh,
        in_specs=placed,
        out_specs=P("section", None, "seq", None, None),
        check_vma=False,
    )
```
